128 devices in a mesh: gx: 8 (over y, core), gy: 16 (over z, x).
Axes of the slice: x: 4, y: 4, z: 4, core: 2. Of those that a mesh axis runs over, the one named last changes fastest.
Arguments:
- thermal_anomaly: float32 [32, 256, 2048], P(None, 'gx', 'gy'), may hold values from -6 to 6
- ambient_diffusion: bfloat16 [256, 2048], P('gx', 'gy'), may hold values from 0.019897461 to 0.25
- solar_light: bfloat16 [256, 2048], P('gx', 'gy'), may hold values from 0.5 to 4
- sea_tile_flags: int32 [8, 16, 64], P('gx', 'gy'), may hold values 0 or 1
- flooded_layer_tally: int32 [8, 16, 64], P('gx', 'gy'), may hold values from 1 to 32
- tile_holder_rank: int32 [8, 16, 64, 1], P('gx', 'gy'), may hold values from 0 to 15; in each aligned block of 64 rows (0 to 63, 64 to 127, ..., all dimensions but the last counted through in order) at most 8 rows name the same one
- solute_amounts: float32 [8, 16, 128, 8, 2048], P('gx', 'gy'), may hold values from 0.09 to 11
- reaction_rates: float32 [8, 8], replicated, may hold values from -0.2 to 0.5
Outputs:
- thermal_final: float32 [32, 256, 2048], P(None, 'gx', 'gy')
- solute_final: float32 [8, 16, 128, 8, 2048], P('gx', 'gy')
The draws below stay inside these ranges and needn't reach their ends.
Inputs may be any that keep to these rules, and one draw needn't show every extreme that they name: `tile_holder_rank`: among the 64 blocks of one device, at most 8 name the same owner, a bound that some block reaches of them.
All inputs are finite; a program needn't handle non-finite values. No bound on the sum of `sea_tile_flags` on one device may be relied on, other than what follows from the above.
Results may differ from the reference program's by a relative error of at most 0.0003.
Values may be sent and summed in bfloat16 or wider, within the bound.
A program may use at most 128 MiB of HBM per device.

```python
import math
import jax
import jax.numpy as jnp
import numpy as np
from jax import lax

VERTICAL_LAYERS = 32
TRACER_COUNT = 8
TILES_EAST = 4
TILES_NORTH = 16
GRID_WIDTH_EAST = 256
GRID_WIDTH_NORTH = 2048
SLOT_CAPACITY = 8
SLOTS = 128
LCOL = 2048
N_GX = 8
N_GY = 16


def draw_solute_amounts(key, part):
    key_level = jax.random.fold_in(key, 11)
    key_cells = jax.random.fold_in(key, 12)
    device_total = N_GX * N_GY
    flat_index = (lax.broadcasted_iota(jnp.int32, (N_GX, N_GY, 1, 1, 1), 0) * N_GY + lax.broadcasted_iota(jnp.int32, (N_GX, N_GY, 1, 1, 1), 1)).astype(jnp.float32)
    ramp_pos = flat_index / float(max(device_total - 1, 1)) - 0.5
    full_shape = (N_GX, N_GY, SLOTS, TRACER_COUNT, LCOL)
    level_noise = jax.random.uniform(key_level, (N_GX, N_GY, 1, TRACER_COUNT, 1), jnp.float32, -0.7, 0.7)
    dev_level = jnp.exp(level_noise + math.log(3.0) * ramp_pos)
    cell_factor = jnp.exp(jax.random.uniform(key_cells, full_shape, jnp.float32, math.log(0.5), math.log(2.0)))
    return dev_level * cell_factor


def touch_ends(entries, key, least, top_value):
    longest = entries.shape.index(max(entries.shape))
    spots = []
    for shift in (0, 1):
        where = [jax.random.randint(jax.random.fold_in(key, axis), (), 0, length) for axis, length in enumerate(entries.shape)]
        where[longest] = (where[longest] + shift) % entries.shape[longest]
        spots.append(tuple(where))
    return entries.at[spots[0]].set(least).at[spots[1]].set(top_value)


def shard_levels(key, dims, shards, low, top_value):
    def one(position, parts):
        heights = jax.random.uniform(jax.random.fold_in(jax.random.fold_in(key, 6), position), (parts,), jnp.float32, low / len(shards), top_value / len(shards))
        return jnp.repeat(jnp.exp(heights), dims[position] // parts).reshape((-1,) + (1,) * (len(dims) - position - 1))

    level = one(*shards[0])
    for cut in shards[1:]:
        level = level * one(*cut)
    return level


def shared_out(stream_key, own, number, rows, count, top, reach, lean):
    order = jax.random.permutation(stream_key, count)
    heavy_load, ordinary = portions_of(count, rows * top, reach, lean, True), portions_of(count, rows * top, reach, lean, False)
    places = jnp.arange(count)

    def named(tallies, turn):
        used = int((tallies > 0).sum())
        fixed = max(1, used // 4)
        shifted = fixed + (places - fixed + turn * (used - fixed)) % max(1, count - fixed)
        return jnp.zeros((count,), jnp.int32).at[order[jnp.where(places < fixed, places, shifted)]].set(jnp.asarray(tallies, jnp.int32))

    tallies = jnp.where(number % 4 == 0, named(heavy_load, number // 4), named(ordinary, number - number // 4 - 1))
    mixed = jax.random.permutation(jax.random.fold_in(own, 3), count)
    source_of, taker = mixed[0:count // 2 * 2:2], mixed[1:count // 2 * 2:2]
    margin = jnp.minimum(tallies[source_of] - 1, reach - tallies[taker]) // 2
    margin = jnp.where((source_of == order[0]) | (taker == order[0]) | (tallies[taker] == 0), 0, jnp.maximum(margin, 0))
    shifted = jax.random.randint(jax.random.fold_in(own, 4), (count // 2,), 0, 1 << 20) % (margin + 1)
    tallies = tallies.at[source_of].add(-shifted).at[taker].add(shifted)
    labels = jnp.searchsorted(jnp.cumsum(tallies), jnp.arange(rows * top), side="right").astype(jnp.int32)
    listing = labels.reshape(top, rows).T
    listing = listing[jax.random.permutation(jax.random.fold_in(own, 1), rows)]
    turn = jax.random.randint(jax.random.fold_in(own, 2), (rows, 1), 0, top)
    return jnp.take_along_axis(listing, (jnp.arange(top)[None, :] + turn) % top, axis=1)


def portions_of(count, total, limit, lean, full):
    weights = [(1 << 20) // math.isqrt(grade ** lean) + 1 for grade in range(1, count + 1)]
    largest = limit if full else min(limit, max(-(-total // count), total * weights[0] // sum(weights)))
    least = 1 if total - largest >= count - 1 else 0
    counts, spare = [largest] + [least] * (count - 1), total - largest - least * (count - 1)
    while spare > 0:
        movable = [i for i in range(1, count) if counts[i] < largest] or [i for i in range(1, count) if counts[i] < limit]
        whole, remaining = sum([weights[i] for i in movable]), spare
        for i in movable:
            addition = min(limit - counts[i], max(1, remaining * weights[i] // whole), spare)
            counts[i] = counts[i] + addition
            spare = spare - addition
    return np.array(counts)


def normal_values(own_key, dims, scale, bound, pieces=(), held_as=jnp.bfloat16):
    loudness = shard_levels(own_key, dims, pieces, -0.22, 0.18) if pieces else 1.0
    result = jax.random.normal(own_key, dims, jnp.float32) * scale * loudness
    return jnp.minimum(jnp.maximum(result, -bound), bound).astype(held_as)


def setup_inputs(seed: int = 0) -> dict:
    key_list = jax.random.split(jax.random.key(seed), 9)
    thermal_anomaly = normal_values(key_list[0], (VERTICAL_LAYERS, GRID_WIDTH_EAST, GRID_WIDTH_NORTH), 1.0, 6.0, ((1, 8), (2, 16)), jnp.float32)
    ambient_diffusion = jnp.clip(jnp.exp(math.log(0.25) - 2.5308688 * jax.random.uniform(key_list[1], (GRID_WIDTH_EAST, GRID_WIDTH_NORTH), jnp.float32) ** shard_levels(key_list[1], (GRID_WIDTH_EAST, GRID_WIDTH_NORTH), ((0, 8), (1, 16)), -0.2, 0.2)), 0.019897461, 0.25).astype(jnp.bfloat16)
    solar_light = jnp.clip(jnp.exp(math.log(4.0) - 2.0794415 * jax.random.uniform(key_list[2], (GRID_WIDTH_EAST, GRID_WIDTH_NORTH), jnp.float32) ** shard_levels(key_list[2], (GRID_WIDTH_EAST, GRID_WIDTH_NORTH), ((0, 8), (1, 16)), -0.2, 0.2)), 0.5, 4.0).astype(jnp.bfloat16)
    sea_tile_flags = touch_ends((jax.random.randint(key_list[3], (N_GX, N_GY, TILES_EAST * TILES_NORTH), 0, 8) < 7).astype(jnp.int32), jax.random.fold_in(key_list[3], 1), 0, 1)
    flooded_layer_tally = touch_ends(jax.random.randint(key_list[4], (N_GX, N_GY, TILES_EAST * TILES_NORTH), 1, VERTICAL_LAYERS + 1), jax.random.fold_in(key_list[4], 1), 1, VERTICAL_LAYERS).astype(jnp.int32)
    tile_holder_rank_keys = jax.random.split(jax.random.fold_in(key_list[5], 1), N_GX * N_GY * (TILES_EAST * TILES_NORTH) // (TILES_EAST * TILES_NORTH))
    tile_holder_rank_turns = jax.random.permutation(jax.random.fold_in(key_list[5], 3), N_GX * N_GY * (TILES_EAST * TILES_NORTH) // (TILES_EAST * TILES_NORTH))
    tile_holder_rank = jax.vmap(lambda own, number: shared_out(jax.random.fold_in(key_list[5], 2), own, number, TILES_EAST * TILES_NORTH, N_GY, 1, SLOT_CAPACITY, 2))(tile_holder_rank_keys, tile_holder_rank_turns).reshape((N_GX, N_GY, TILES_EAST * TILES_NORTH, 1))
    solute_amounts = draw_solute_amounts(jax.random.fold_in(key_list[8], 71), 0)
    reaction_rates = jnp.clip(jax.random.uniform(key_list[7], (TRACER_COUNT, TRACER_COUNT), jnp.float32, -0.2, 0.5), -0.2, 0.5)
    return dict(thermal_anomaly=thermal_anomaly, ambient_diffusion=ambient_diffusion, solar_light=solar_light, sea_tile_flags=sea_tile_flags, flooded_layer_tally=flooded_layer_tally, tile_holder_rank=tile_holder_rank, solute_amounts=solute_amounts, reaction_rates=reaction_rates)


NU_COEF = 0.2
STEP_DT = 0.05
ATTEN_WATER = 0.06
ATTEN_CHL = 0.05
WARMING_SCALE = 0.5
GROWTH_TEMP = 0.063


def masked_step(field, within_layer):
    center = field[:, 1:-1, 1:-1]
    span_east = center.shape[1]
    span_north = center.shape[2]
    total = jnp.zeros_like(center)
    for first, second in ((0, 1), (2, 1), (1, 0), (1, 2)):
        near = field[:, first:first + span_east, second:second + span_north]
        total = total + within_layer[:, first:first + span_east, second:second + span_north] * (near - center)
    return center + NU_COEF * within_layer[:, 1:-1, 1:-1] * total


def diffusion_mixer(temp_b, kbg_b):
    below = jnp.concatenate([temp_b[..., 1:, :], temp_b[..., -1:, :]], axis=-2)
    return (kbg_b[..., None, :] * (1.0 + 0.5 * jnp.tanh(temp_b - below))).astype(jnp.bfloat16)


def validity(tile_amount):
    levels = lax.broadcasted_iota(jnp.int32, (1, VERTICAL_LAYERS, 1), 1)
    valid = (levels < tile_amount[:, None, None]).astype(jnp.float32)
    active = (levels + 1 < tile_amount[:, None, None]).astype(jnp.float32)
    return valid, active


def totals(amounts_on_chip, valid):
    return jnp.sum(amounts_on_chip * valid[:, None], axis=(0, 2, 3))


def column_step(temp_b, kappa_b, sw_b, tile_amount, amounts_on_chip, reaction_rates):
    valid, active = validity(tile_amount)
    atten = ATTEN_WATER + ATTEN_CHL * amounts_on_chip[:, 0]
    cumul = jnp.cumsum(atten, axis=1)
    surface = sw_b.astype(jnp.float32)[:, None, :]
    top = surface * jnp.exp(-(cumul - atten))
    bottom = surface * jnp.exp(-cumul)
    heat = (valid * (top - bottom)).astype(jnp.bfloat16)
    growth = jnp.exp(GROWTH_TEMP * temp_b.astype(jnp.float32)) * top / (top + 1.0)
    mixed = jnp.einsum("rs,nslc->nrlc", reaction_rates, amounts_on_chip, precision=lax.Precision.HIGHEST)
    below = jnp.concatenate([amounts_on_chip[:, :, 1:], amounts_on_chip[:, :, -1:]], axis=2)
    flux = (kappa_b.astype(jnp.float32) * active)[:, None] * (below - amounts_on_chip)
    above = jnp.concatenate([jnp.zeros_like(flux[:, :, :1]), flux[:, :, :-1]], axis=2)
    new = amounts_on_chip + valid[:, None] * STEP_DT * (flux - above + growth[:, None] * mixed)
    return new, heat


def cells_of(per_block):
    grid = per_block.reshape(N_GX, N_GY, TILES_EAST, TILES_NORTH).transpose(0, 2, 1, 3).reshape(N_GX * TILES_EAST, N_GY * TILES_NORTH)
    return jnp.repeat(jnp.repeat(grid, 8, axis=0), 8, axis=1)


def blocks_2d(field):
    return field.reshape(N_GX, TILES_EAST, 8, N_GY, TILES_NORTH, 8).transpose(0, 3, 1, 4, 2, 5).reshape(N_GX, N_GY, TILES_EAST * TILES_NORTH, 64)


def reference(thermal_anomaly, ambient_diffusion, solar_light, sea_tile_flags, flooded_layer_tally, tile_holder_rank, solute_amounts, reaction_rates):
    depth_block = sea_tile_flags * flooded_layer_tally
    cell_count = cells_of(depth_block)
    level_idx = lax.broadcasted_iota(jnp.int32, (VERTICAL_LAYERS, 1, 1), 0)
    within_layer = (level_idx < cell_count[None]).astype(jnp.float32)
    piled_tiles = jnp.pad(jnp.stack([thermal_anomaly, within_layer]), ((0, 0), (0, 0), (1, 1), (1, 1)))
    advanced_verticals = masked_step(piled_tiles[0], piled_tiles[1])
    dispatched = advanced_verticals.astype(jnp.bfloat16)
    thermal_tiles = dispatched.reshape(VERTICAL_LAYERS, N_GX, TILES_EAST, 8, N_GY, TILES_NORTH, 8).transpose(1, 4, 2, 5, 0, 3, 6).reshape(N_GX, N_GY, TILES_EAST * TILES_NORTH, VERTICAL_LAYERS, 64)
    ambient_diffusion_tiles = blocks_2d(ambient_diffusion)
    shortwave_blocks = blocks_2d(solar_light)
    diffusion_each_tile = diffusion_mixer(thermal_tiles.astype(jnp.float32), ambient_diffusion_tiles.astype(jnp.float32))
    holder_chip = tile_holder_rank[..., 0]
    order = jnp.arange(TILES_EAST * TILES_NORTH, dtype=jnp.int32)
    same = (holder_chip[..., :, None] == holder_chip[..., None, :]) & (order[None, :] < order[:, None])
    rank = jnp.sum(same.astype(jnp.int32), axis=-1)
    position_rank = (jnp.arange(N_GY, dtype=jnp.int32)[None, :, None] * SLOT_CAPACITY + rank).astype(jnp.int32)
    tile_line = jnp.broadcast_to(jnp.arange(N_GX, dtype=jnp.int32)[:, None, None], holder_chip.shape)
    position_summation = N_GY * SLOT_CAPACITY
    compact_warmth = jnp.zeros((N_GX, N_GY, position_summation, VERTICAL_LAYERS, 64), jnp.bfloat16).at[tile_line, holder_chip, position_rank].set(thermal_tiles)
    compact_diffusion = jnp.zeros((N_GX, N_GY, position_summation, VERTICAL_LAYERS, 64), jnp.bfloat16).at[tile_line, holder_chip, position_rank].set(diffusion_each_tile)
    packed_shortwave = jnp.zeros((N_GX, N_GY, position_summation, 64), jnp.bfloat16).at[tile_line, holder_chip, position_rank].set(shortwave_blocks)
    packed_level_count = jnp.zeros((N_GX, N_GY, position_summation), jnp.int32).at[tile_line, holder_chip, position_rank].set(depth_block)
    concentration_global = solute_amounts.reshape(N_GX, N_GY * position_summation, TRACER_COUNT, VERTICAL_LAYERS, 64)

    def owner_pass(items):
        temp_b, kappa_b, sw_b, tile_amount, amounts_on_chip = items
        valid, active = validity(tile_amount)
        new, heat = column_step(temp_b, kappa_b, sw_b, tile_amount, amounts_on_chip, reaction_rates)
        return new, heat, totals(amounts_on_chip, valid), totals(new, valid), jnp.sum(valid) * 64.0

    updated_global, heat_global, old_parts, new_parts, cell_parts = lax.map(owner_pass, (
        compact_warmth.reshape(N_GX, N_GY * position_summation, VERTICAL_LAYERS, 64), compact_diffusion.reshape(N_GX, N_GY * position_summation, VERTICAL_LAYERS, 64),
        packed_shortwave.reshape(N_GX, N_GY * position_summation, 64), packed_level_count.reshape(N_GX, N_GY * position_summation), concentration_global))
    old_total = jnp.sum(old_parts, axis=0)
    new_total = jnp.sum(new_parts, axis=0)
    cells = jnp.sum(cell_parts)
    shift = (old_total - new_total) / jnp.maximum(cells, 1.0)

    def totals_corrected(items):
        new, amounts_on_chip, tile_amount = items
        valid, active = validity(tile_amount)
        return jnp.where(valid[:, None] > 0, new + shift[None, :, None, None], amounts_on_chip)

    solute_final = lax.map(totals_corrected, (updated_global, concentration_global, packed_level_count.reshape(N_GX, N_GY * position_summation)))
    solute_final = solute_final.reshape(solute_amounts.shape)
    heat_in_slots = heat_global.reshape(N_GX, N_GY, position_summation, VERTICAL_LAYERS, 64)
    heat_blocks = heat_in_slots[tile_line, holder_chip, position_rank]
    warming_each_site = heat_blocks.reshape(N_GX, N_GY, TILES_EAST, TILES_NORTH, VERTICAL_LAYERS, 8, 8).transpose(4, 0, 2, 5, 1, 3, 6).reshape(VERTICAL_LAYERS, N_GX * TILES_EAST * 8, N_GY * TILES_NORTH * 8)
    thermal_final = advanced_verticals + WARMING_SCALE * warming_each_site.astype(jnp.float32)
    return thermal_final, solute_final
```

```python
import functools

import jax
import jax.numpy as jnp
from jax import lax
from jax.experimental import pallas as pl
from jax.experimental.pallas import tpu as pltpu
from jax.sharding import PartitionSpec as P

MESH = pl.DeviceIdType.MESH
F32 = jnp.float32
BF16 = jnp.bfloat16

NU_COEF = 0.2
STEP_DT = 0.05
ATTEN_WATER = 0.06
ATTEN_CHL = 0.05
WARMING_SCALE = 0.5
GROWTH_TEMP = 0.063

LEVELS = 32
BLOCKS = 64
ROWS = 144
NT = (((1,), (1,)), ((), ()))
TN = (((0,), (0,)), ((), ()))


def iota(shape, dim):
    return lax.broadcasted_iota(jnp.int32, shape, dim)


def one_hot(mask):
    return jnp.where(mask, 1.0, 0.0).astype(BF16)


def swap_chunks(parts):
    lane = iota(parts[0].shape, 1)
    low = lane < 64
    even = (lane & 32) == 0
    a, b, c, d = parts
    a, c = jnp.where(low, a, pltpu.roll(c, 64, 1)), jnp.where(low, pltpu.roll(a, 64, 1), c)
    b, d = jnp.where(low, b, pltpu.roll(d, 64, 1)), jnp.where(low, pltpu.roll(b, 64, 1), d)
    a, b = jnp.where(even, a, pltpu.roll(b, 32, 1)), jnp.where(even, pltpu.roll(a, 96, 1), b)
    c, d = jnp.where(even, c, pltpu.roll(d, 32, 1)), jnp.where(even, pltpu.roll(c, 96, 1), d)
    return [a, b, c, d]


def exchange_kernel(
    gx_n,
    gy_n,
    t_ref,
    amb_ref,
    light_ref,
    flag_ref,
    tally_ref,
    hold_ref,
    rate_ref,
    c_hbm,
    pre_ref,
    cnt_ref,
    shift_ref,
    therm_ref,
    c_ref,
    sel_ref,
    ut_ref,
    step_ref,
    pay_ref,
    recv_ref,
    hs_ref,
    hr_ref,
    tmp_ref,
    heat_ref,
    kap_ref,
    gv_ref,
    mix_ref,
    gsum_ref,
    warm_ref,
    hxs_ref,
    hxr_ref,
    hys_ref,
    hyr_ref,
    ar_ref,
    ara_ref,
    arb_ref,
    c_sem,
    halo_s,
    halo_r,
    fs_sem,
    fr_sem,
    own_sem,
    bs_sem,
    br_sem,
    as_sem,
    ar_sem,
    gs_sem,
    gr_sem,
):
    nz = gy_n // 4
    mx = lax.axis_index("gx")
    my = lax.axis_index("gy")
    mz = my // 4
    mq = my % 4

    def c_copy(z):
        return pltpu.make_async_copy(
            c_hbm.at[pl.ds(z * 32, 32)], c_ref.at[pl.ds(z * 32, 32)], c_sem.at[z]
        )

    for q in range(nz):
        c_copy((mz - q + nz) % nz).start()

    bar = pltpu.get_barrier_semaphore()
    for d in range(1, gx_n):
        pl.semaphore_signal(
            bar, 1, device_id={"gx": (mx + d) % gx_n}, device_id_type=MESH
        )
    for d in range(1, gy_n):
        pl.semaphore_signal(
            bar, 1, device_id={"gy": (my + d) % gy_n}, device_id_type=MESH
        )

    dep = (flag_ref[...] * tally_ref[...]).astype(F32)
    hold = hold_ref[...].astype(F32)
    bi = iota((BLOCKS, BLOCKS), 0)
    bj = iota((BLOCKS, BLOCKS), 1)
    hold_b = jnp.broadcast_to(hold, (BLOCKS, BLOCKS))
    hold_c = jnp.sum(jnp.where(bi == bj, hold_b, 0.0), axis=1, keepdims=True)
    same = jnp.where((hold_c == hold_b) & (bi < bj), 1.0, 0.0)
    rank = jnp.sum(same, axis=0, keepdims=True)
    slot = hold * 8.0 + rank
    r8 = iota((8, BLOCKS), 0)
    pair = jnp.where(
        r8 == 0,
        jnp.broadcast_to(slot, (8, BLOCKS)),
        jnp.where(r8 == 1, jnp.broadcast_to(dep, (8, BLOCKS)), 0.0),
    ).astype(BF16)
    spread = one_hot(iota((BLOCKS, 512), 0) == (iota((BLOCKS, 512), 1) >> 3))
    lanes = jnp.dot(pair, spread, preferred_element_type=F32)
    slot_l = lanes[0:1]
    dep_l = lanes[1:2]
    lane8 = iota((8, 128), 1)
    dep_b = [
        jnp.broadcast_to(dep_l[:, 128 * bx : 128 * bx + 128], (8, 128)) for bx in range(4)
    ]
    cells = jnp.sum(dep, axis=1, keepdims=True) * 64.0

    hxs_ref[0, 0:32, :] = t_ref[:, 0, :]
    hxs_ref[1, 0:32, :] = t_ref[:, 31, :]
    hxs_ref[0, 32:40, :] = dep_b[0]
    hxs_ref[1, 32:40, :] = dep_b[3]

    def pack_edges(k, acc):
        low, high = acc
        low = pltpu.roll(low, 127, 1)
        high = pltpu.roll(high, 127, 1)
        for bx in range(4):
            part = t_ref[k, 8 * bx : 8 * bx + 8, :]
            place = 32 * bx + 31
            low = jnp.where(lane8 == place, pltpu.roll(part, place, 1), low)
            high = jnp.where(lane8 == place, pltpu.roll(part, (place + 1) % 128, 1), high)
        return low, high

    zero8 = jnp.zeros((8, 128), F32)
    low, high = lax.fori_loop(0, LEVELS, pack_edges, (zero8, zero8))
    dlow, dhigh = zero8, zero8
    for bx in range(4):
        dlow = jnp.where(lane8 == 32 * bx, pltpu.roll(dep_b[bx], 32 * bx, 1), dlow)
        dhigh = jnp.where(lane8 == 32 * bx, pltpu.roll(dep_b[bx], 32 * bx + 1, 1), dhigh)
    hys_ref[0, 0:8, :] = low
    hys_ref[1, 0:8, :] = high
    hys_ref[0, 8:16, :] = dlow
    hys_ref[1, 8:16, :] = dhigh

    pl.semaphore_wait(bar, gx_n - 1 + gy_n - 1)

    def halo(side):
        step = gx_n - 1 if side == 0 else 1
        stepy = gy_n - 1 if side == 0 else 1
        return (
            pltpu.make_async_remote_copy(
                hxs_ref.at[side],
                hxr_ref.at[1 - side],
                halo_s.at[side],
                halo_r.at[side],
                device_id={"gx": (mx + step) % gx_n},
                device_id_type=MESH,
            ),
            pltpu.make_async_remote_copy(
                hys_ref.at[side],
                hyr_ref.at[1 - side],
                halo_s.at[2 + side],
                halo_r.at[2 + side],
                device_id={"gy": (my + stepy) % gy_n},
                device_id_type=MESH,
            ),
        )

    halos = halo(0) + halo(1)
    for copy in halos:
        copy.start()

    lane_n = iota((1, 512), 1)
    key_l = slot_l * 8.0 + (lane_n & 7).astype(F32)

    def build_sel(z, carry):
        m = iota((256, 1), 0) + z * 256
        key = ((m >> 6) << 6) | ((m & 7) << 3) | ((m >> 3) & 7)
        sel_ref[pl.ds(pl.multiple_of(z * 256, 256), 256), :] = one_hot(
            jnp.broadcast_to(key.astype(F32), (256, 512))
            == jnp.broadcast_to(key_l, (256, 512))
        )
        return carry

    lax.fori_loop(0, nz, build_sel, 0)

    def by_lanes(field):
        return jnp.concatenate([field[8 * bx : 8 * bx + 8] for bx in range(4)], axis=1)

    aux = jnp.concatenate(
        [
            by_lanes(light_ref[...].astype(F32)),
            by_lanes(amb_ref[...].astype(F32)),
            jnp.broadcast_to(dep_l, (8, 512)),
            jnp.zeros((8, 512), F32),
        ],
        axis=0,
    ).astype(BF16)
    er = iota((256, 32), 0)
    ef = iota((256, 32), 1)
    place = one_hot(ef == jnp.where(er < 128, er >> 3, 16))
    wide = jnp.dot(place, aux, preferred_element_type=F32)
    wide = jnp.where(
        (iota((256, 512), 0) & 7) == (iota((256, 512), 1) & 7), wide, 0.0
    ).astype(BF16)
    slots = 8 * gy_n
    sel_b = one_hot(
        iota((slots, 512), 0).astype(F32) == jnp.broadcast_to(slot_l, (slots, 512))
    )
    packed_aux = lax.dot_general(sel_b, wide, NT, preferred_element_type=F32)
    packed_aux = packed_aux.reshape(gy_n, 8, 256)
    pay_ref[:, 128:144, :] = jnp.concatenate(
        [packed_aux[:, :, :128], packed_aux[:, :, 128:]], axis=1
    ).astype(BF16)

    for copy in halos:
        copy.wait_recv()

    row = iota((32, 128), 0)
    lane = iota((32, 128), 1)
    on_low_x = jnp.where(mx > 0, 1.0, 0.0)
    on_high_x = jnp.where(mx < gx_n - 1, 1.0, 0.0)
    on_low_y = jnp.where(my > 0, 1.0, 0.0)
    on_high_y = jnp.where(my < gy_n - 1, 1.0, 0.0)

    def around(field, below_row, above_row, low_h, high_h):
        up = jnp.where(row == 0, below_row, pltpu.roll(field, 1, 0))
        down = jnp.where(row == 31, above_row, pltpu.roll(field, 31, 0))
        low_v = jnp.concatenate(
            [low_h] + [pltpu.roll(low_h, 128 - 32 * bx, 1) for bx in (1, 2, 3)], axis=0
        )
        high_v = jnp.concatenate(
            [pltpu.roll(high_h, 127 - 32 * bx, 1) for bx in range(4)], axis=0
        )
        west = jnp.where(lane == 0, low_v, pltpu.roll(field, 1, 1))
        east = jnp.where(lane == 127, high_v, pltpu.roll(field, 127, 1))
        return up, down, west, east

    dep2 = jnp.concatenate(dep_b, axis=0)
    dep_n = around(
        dep2,
        hxr_ref[0, 32:33, :] * on_low_x,
        hxr_ref[1, 32:33, :] * on_high_x,
        hyr_ref[0, 8:16, :] * on_low_y,
        hyr_ref[1, 8:16, :] * on_high_y,
    )

    def stencil(kk, carry):
        low_h, high_h = carry
        done = []
        for half in range(2):
            k = kk * 2 + half
            field = t_ref[k]
            near = around(
                field,
                hxr_ref[0, pl.ds(k, 1), :],
                hxr_ref[1, pl.ds(k, 1), :],
                low_h,
                high_h,
            )
            low_h = pltpu.roll(low_h, 127, 1)
            high_h = pltpu.roll(high_h, 127, 1)
            kf = k.astype(F32)
            total = jnp.where(dep_n[0] > kf, near[0] - field, 0.0)
            for d, n in zip(dep_n[1:], near[1:]):
                total = total + jnp.where(d > kf, n - field, 0.0)
            stepped = field + NU_COEF * jnp.where(dep2 > kf, total, 0.0)
            step_ref[k] = stepped
            done.append(stepped)
        rows = pl.ds(pl.multiple_of(kk * 16, 16), 16)
        for bx in range(4):
            ut_ref[rows, 128 * bx : 128 * bx + 128] = jnp.concatenate(
                [d[8 * bx : 8 * bx + 8] for d in done], axis=0
            ).astype(BF16)
        return low_h, high_h

    lax.fori_loop(0, LEVELS // 2, stencil, (hyr_ref[0, 0:8, :], hyr_ref[1, 0:8, :]))

    def forward(other):
        return pltpu.make_async_remote_copy(
            pay_ref.at[other],
            recv_ref.at[my],
            fs_sem.at[other],
            fr_sem.at[my],
            device_id={"gy": other},
            device_id_type=MESH,
        )

    def arrival(other):
        return pltpu.make_async_remote_copy(
            pay_ref.at[other],
            recv_ref.at[other],
            fs_sem.at[other],
            fr_sem.at[other],
            device_id={"gy": other},
            device_id_type=MESH,
        )

    own = pltpu.make_async_copy(pay_ref.at[my], recv_ref.at[my], own_sem.at[0])
    for q in range(nz):
        z = (mz + q) % nz
        part = lax.dot_general(
            sel_ref[pl.ds(pl.multiple_of(z * 256, 256), 256), :],
            ut_ref[...],
            NT,
            preferred_element_type=F32,
        ).astype(BF16)
        part = part.reshape(4, 64, 256)
        pay_ref[pl.ds(z * 4, 4), 0:64, :] = part[:, :, :128]
        pay_ref[pl.ds(z * 4, 4), 64:128, :] = part[:, :, 128:]
        for d in range(4):
            if q == 0 and d == 0:
                own.start()
            else:
                forward(z * 4 + (mq + d) % 4).start()

    pi = iota((256, 256), 0)
    po = iota((256, 256), 1)
    to_columns = one_hot(po == (((pi & 31) << 3) | (pi >> 5)))
    from_columns = one_hot(pi == (((po & 31) << 3) | (po >> 5)))
    rates = jnp.concatenate([rate_ref[...]] * 32, axis=0)
    spread_r = (iota((8, 256), 1) & 7) == iota((8, 256), 0)
    rates_hi = rates.astype(BF16)
    rates_lo = (rates - rates_hi.astype(F32)).astype(BF16)
    spread_r = one_hot(spread_r)
    diagonal = (pi >> 3) == (po >> 3)
    mat_hi = jnp.where(
        diagonal, jnp.dot(rates_hi, spread_r, preferred_element_type=F32), 0.0
    ).astype(BF16)
    mat_lo = jnp.where(
        diagonal, jnp.dot(rates_lo, spread_r, preferred_element_type=F32), 0.0
    ).astype(BF16)
    upper = lane >= 64
    upper8 = lane8 >= 64
    gsum_ref[...] = jnp.zeros((8, 128), F32)

    def back(other):
        return pltpu.make_async_remote_copy(
            hs_ref.at[other],
            hr_ref.at[my],
            bs_sem.at[other],
            br_sem.at[my],
            device_id={"gy": other},
            device_id_type=MESH,
        )

    def back_arrival(other):
        return pltpu.make_async_remote_copy(
            hs_ref.at[other],
            hr_ref.at[other],
            bs_sem.at[other],
            br_sem.at[other],
            device_id={"gy": other},
            device_id_type=MESH,
        )

    own_back = pltpu.make_async_copy(hs_ref.at[my], hr_ref.at[my], own_sem.at[1])

    for q in range(nz):
        z = (mz - q + nz) % nz
        s0 = z * 32
        for d in range(4):
            if q == 0 and d == 0:
                own.wait()
            else:
                arrival(z * 4 + (mq - d + 4) % 4).wait_recv()
        c_copy(z).wait()
        blk = recv_ref[pl.ds(z * 4, 4), :, :].astype(F32)
        rows = []
        for h in range(2):
            quads = []
            for yh in range(2):
                quads.append(
                    swap_chunks(
                        [
                            blk[:, h * 64 + y * 8 : h * 64 + y * 8 + 8, :].reshape(32, 128)
                            for y in range(yh * 4, yh * 4 + 4)
                        ]
                    )
                )
            for g in range(4):
                rows.append(jnp.concatenate([quads[0][g], quads[1][g]], axis=1))
        cols = jnp.dot(
            jnp.concatenate(rows, axis=0).astype(BF16),
            to_columns,
            preferred_element_type=F32,
        )
        for g in range(8):
            tmp_ref[:, g * 256 : g * 256 + 256] = cols[g * 32 : g * 32 + 32]

        la = blk[:, 128:136, :].reshape(32, 128)
        cnt = blk[:, 136:144, :].reshape(32, 128)
        cnt_ref[pl.ds(s0, 32), :] = cnt
        la_r = pltpu.roll(la, 64, 1)
        light = jnp.where(upper, la_r, la)
        amb = jnp.where(upper, la, la_r)
        level = jnp.where(upper, 1.0, 0.0)
        run = jnp.zeros((32, 128), F32)
        prev = light
        t_next = tmp_ref[:, 0:128]
        tr_next = pltpu.roll(t_next, 64, 1)
        for i in range(16):
            at = slice(128 * i, 128 * i + 128)
            t_i, tr_i = t_next, tr_next
            if i < 15:
                t_next = tmp_ref[:, 128 * i + 128 : 128 * i + 256]
                tr_next = pltpu.roll(t_next, 64, 1)
                t_below = jnp.where(upper, tr_next, tr_i)
            else:
                t_below = jnp.where(upper, t_i, tr_i)
            atten = ATTEN_WATER + ATTEN_CHL * c_ref[pl.ds(s0, 32), 0, at]
            atten_r = pltpu.roll(atten, 64, 1)
            both = atten + atten_r
            cum = run + jnp.where(upper, both, atten)
            run = run + both
            bottom = light * jnp.exp(-cum)
            bottom_r = pltpu.roll(bottom, 64, 1)
            top = jnp.where(upper, bottom_r, prev)
            prev = bottom_r
            wet = cnt - 2.0 * i > level
            heat_ref[:, at] = jnp.where(wet, top - bottom, 0.0)
            growth = jnp.exp(GROWTH_TEMP * t_i) * top / (top + 1.0)
            gv_ref[i] = jnp.where(wet, STEP_DT * growth, 0.0)
            kap = amb * (1.0 + 0.5 * jnp.tanh(t_i - t_below))
            kap_ref[i] = jnp.where(cnt - (2.0 * i + 1.0) > level, STEP_DT * kap, 0.0)

        heat = jnp.concatenate(
            [heat_ref[:, g * 256 : g * 256 + 256] for g in range(8)], axis=0
        ).astype(BF16)
        back_cols = jnp.dot(heat, from_columns, preferred_element_type=F32)
        for h in range(2):
            quads = [
                swap_chunks(
                    [
                        back_cols[
                            (h * 4 + g) * 32 : (h * 4 + g) * 32 + 32, yh * 128 : yh * 128 + 128
                        ]
                        for g in range(4)
                    ]
                )
                for yh in range(2)
            ]
            flat = [p.reshape(4, 8, 128) for p in quads[0] + quads[1]]
            for y in range(0, 8, 2):
                hs_ref[pl.ds(z * 4, 4), h * 64 + y * 8 : h * 64 + y * 8 + 16, :] = (
                    jnp.concatenate([flat[y], flat[y + 1]], axis=1).astype(BF16)
                )
        for d in range(4):
            if q == 0 and d == 0:
                own_back.start()
            else:
                back(z * 4 + (mq - d + 4) % 4).start()

        for g in range(8):
            at = slice(256 * g, 256 * g + 256)
            c_b = c_ref[pl.ds(s0, 32), :, at].reshape(256, 256).astype(BF16)
            mix_ref[:, at] = jnp.dot(mat_hi, c_b, preferred_element_type=F32) + jnp.dot(
                mat_lo, c_b, preferred_element_type=F32
            )

        def tracers(s, acc):
            c_next = c_ref[s0 + s, :, 0:128]
            cr_next = pltpu.roll(c_next, 64, 1)
            fr_prev = jnp.zeros((8, 128), F32)
            for i in range(16):
                at = slice(128 * i, 128 * i + 128)
                c_i, cr_i = c_next, cr_next
                if i < 15:
                    c_next = c_ref[s0 + s, :, 128 * i + 128 : 128 * i + 256]
                    cr_next = pltpu.roll(c_next, 64, 1)
                below = jnp.where(upper8, cr_next, cr_i)
                flux = kap_ref[i, pl.ds(s, 1), :] * (below - c_i)
                flux_r = pltpu.roll(flux, 64, 1)
                above = jnp.where(upper8, flux_r, fr_prev)
                fr_prev = flux_r
                grown = (
                    gv_ref[i, pl.ds(s, 1), :]
                    * mix_ref[pl.ds(pl.multiple_of(s * 8, 8), 8), at]
                )
                acc = acc + grown
                pre_ref[s0 + s, :, at] = c_i + ((flux - above) + grown)
            return acc

        gsum_ref[...] = lax.fori_loop(0, 32, tracers, gsum_ref[...])

    ar_ref[0, 0:8, :] = gsum_ref[...]
    ar_ref[0, 8:16, :] = jnp.broadcast_to(cells, (8, 128))

    def gx_send(other):
        return pltpu.make_async_remote_copy(
            ar_ref.at[0],
            ara_ref.at[mx],
            as_sem.at[other],
            ar_sem.at[mx],
            device_id={"gx": other},
            device_id_type=MESH,
        )

    def gx_arrival(other):
        return pltpu.make_async_remote_copy(
            ar_ref.at[0],
            ara_ref.at[other],
            as_sem.at[other],
            ar_sem.at[other],
            device_id={"gx": other},
            device_id_type=MESH,
        )

    def gy_send(other):
        return pltpu.make_async_remote_copy(
            ar_ref.at[1],
            arb_ref.at[my],
            gs_sem.at[other],
            gr_sem.at[my],
            device_id={"gy": other},
            device_id_type=MESH,
        )

    def gy_arrival(other):
        return pltpu.make_async_remote_copy(
            ar_ref.at[1],
            arb_ref.at[other],
            gs_sem.at[other],
            gr_sem.at[other],
            device_id={"gy": other},
            device_id_type=MESH,
        )

    for d in range(1, gx_n):
        gx_send((mx + d) % gx_n).start()
    ara_ref[mx] = ar_ref[0]
    for d in range(1, gx_n):
        gx_arrival((mx + d) % gx_n).wait_recv()
    ar_ref[1] = jnp.sum(ara_ref[...], axis=0)
    for d in range(1, gy_n):
        gy_send((my + d) % gy_n).start()
    arb_ref[my] = ar_ref[1]

    for q in range(nz):
        z = (mz + q) % nz
        for d in range(4):
            if q == 0 and d == 0:
                own_back.wait()
            else:
                back_arrival(z * 4 + (mq + d) % 4).wait_recv()
        got = hr_ref[pl.ds(z * 4, 4), :, :]
        sel = sel_ref[pl.ds(pl.multiple_of(z * 256, 256), 256), :]
        for h in range(2):
            lhs = got[:, h * 64 : h * 64 + 64, :].reshape(256, 128)
            warm = lax.dot_general(lhs, sel, TN, preferred_element_type=F32)
            rows_h = slice(128 * h, 128 * h + 128)
            if q == 0:
                warm_ref[rows_h, :] = warm
            else:
                warm_ref[rows_h, :] = warm_ref[rows_h, :] + warm

    def finish(k, carry):
        part = warm_ref[pl.ds(pl.multiple_of(k * 8, 8), 8), :]
        for bx in range(4):
            therm_ref[k, 8 * bx : 8 * bx + 8, :] = (
                step_ref[k, 8 * bx : 8 * bx + 8, :]
                + WARMING_SCALE * part[:, 128 * bx : 128 * bx + 128]
            )
        return carry

    lax.fori_loop(0, LEVELS, finish, 0)

    for d in range(1, gy_n):
        gy_arrival((my + d) % gy_n).wait_recv()
    total = jnp.sum(arb_ref[...], axis=0)
    grown = jnp.sum(total[0:8], axis=1, keepdims=True)
    shift_ref[...] = -(jnp.broadcast_to(grown, (8, 128)) / jnp.maximum(total[8:16], 1.0))

    for copy in halos:
        copy.wait_send()
    for d in range(1, gy_n):
        forward((my + d) % gy_n).wait_send()
        back((my + d) % gy_n).wait_send()
        gy_send((my + d) % gy_n).wait_send()
    for d in range(1, gx_n):
        gx_send((mx + d) % gx_n).wait_send()


def finish_kernel(pre_ref, cnt_ref, shift_ref, therm_ref, out_ref, thout_ref, buf_ref, sem):
    upper = iota((8, 128), 1) >= 64
    level = jnp.where(upper, 1.0, 0.0)
    n = pre_ref.shape[0] // 16
    thermal = pltpu.make_async_copy(therm_ref, thout_ref, sem.at[2])
    thermal.start()
    shift = shift_ref[...]

    def out_copy(c):
        return pltpu.make_async_copy(
            buf_ref.at[c % 2], out_ref.at[pl.ds(c * 16, 16)], sem.at[c % 2]
        )

    for c in range(n):
        if c >= 2:
            out_copy(c - 2).wait()

        def one(s, carry):
            cnt = cnt_ref[pl.ds(c * 16 + s, 1), :]
            for i in range(16):
                at = slice(128 * i, 128 * i + 128)
                buf_ref[c % 2, s, :, at] = pre_ref[c * 16 + s, :, at] + jnp.where(
                    cnt - 2.0 * i > level, shift, 0.0
                )
            return carry

        lax.fori_loop(0, 16, one, 0)
        out_copy(c).start()
    for c in range(max(n - 2, 0), n):
        out_copy(c).wait()
    thermal.wait()


def solution(mesh):
    gx_n = mesh.shape["gx"]
    gy_n = mesh.shape["gy"]
    slots = 8 * gy_n

    def on_device(thermal, amb, light, flags, tally, hold, solutes, rates):
        dma = pltpu.SemaphoreType.DMA
        vmem = pl.BlockSpec(memory_space=pltpu.VMEM)
        hbm = pl.BlockSpec(memory_space=pl.ANY)
        tracers = solutes.reshape(slots, 8, 2048)
        pre, cnt, shift, therm = pl.pallas_call(
            functools.partial(exchange_kernel, gx_n, gy_n),
            out_shape=[
                pltpu.VMEM((slots, 8, 2048), F32),
                pltpu.VMEM((slots, 128), F32),
                pltpu.VMEM((8, 128), F32),
                pltpu.VMEM((32, 32, 128), F32),
            ],
            in_specs=[vmem] * 7 + [hbm],
            out_specs=[vmem] * 4,
            scratch_shapes=[
                pltpu.VMEM((slots, 8, 2048), F32),
                pltpu.VMEM((64 * gy_n, 512), BF16),
                pltpu.VMEM((256, 512), BF16),
                pltpu.VMEM((32, 32, 128), F32),
                pltpu.VMEM((gy_n, ROWS, 128), BF16),
                pltpu.VMEM((gy_n, ROWS, 128), BF16),
                pltpu.VMEM((gy_n, 128, 128), BF16),
                pltpu.VMEM((gy_n, 128, 128), BF16),
                pltpu.VMEM((32, 2048), F32),
                pltpu.VMEM((32, 2048), F32),
                pltpu.VMEM((16, 32, 128), F32),
                pltpu.VMEM((16, 32, 128), F32),
                pltpu.VMEM((256, 2048), F32),
                pltpu.VMEM((8, 128), F32),
                pltpu.VMEM((256, 512), F32),
                pltpu.VMEM((2, 40, 128), F32),
                pltpu.VMEM((2, 40, 128), F32),
                pltpu.VMEM((2, 16, 128), F32),
                pltpu.VMEM((2, 16, 128), F32),
                pltpu.VMEM((2, 16, 128), F32),
                pltpu.VMEM((gx_n, 16, 128), F32),
                pltpu.VMEM((gy_n, 16, 128), F32),
                dma((gy_n // 4,)),
                dma((4,)),
                dma((4,)),
                dma((gy_n,)),
                dma((gy_n,)),
                dma((2,)),
                dma((gy_n,)),
                dma((gy_n,)),
                dma((gx_n,)),
                dma((gx_n,)),
                dma((gy_n,)),
                dma((gy_n,)),
            ],
            compiler_params=pltpu.CompilerParams(
                collective_id=0, has_side_effects=True, vmem_limit_bytes=40 * 1024 * 1024
            ),
            name="exchange",
        )(
            thermal,
            amb,
            light,
            flags.reshape(1, BLOCKS),
            tally.reshape(1, BLOCKS),
            hold.reshape(1, BLOCKS),
            rates,
            tracers,
        )
        out, therm_out = pl.pallas_call(
            finish_kernel,
            out_shape=[
                jax.ShapeDtypeStruct((slots, 8, 2048), F32),
                jax.ShapeDtypeStruct((32, 32, 128), F32),
            ],
            in_specs=[vmem] * 4,
            out_specs=[hbm] * 2,
            scratch_shapes=[pltpu.VMEM((2, 16, 8, 2048), F32), dma((3,))],
            compiler_params=pltpu.CompilerParams(vmem_limit_bytes=16 * 1024 * 1024),
            name="finish",
        )(pre, cnt, shift, therm)
        return therm_out, out.reshape(solutes.shape)

    return jax.shard_map(
        on_device,
        mesh=mesh,
        in_specs=(
            P(None, "gx", "gy"),
            P("gx", "gy"),
            P("gx", "gy"),
            P("gx", "gy", None),
            P("gx", "gy", None),
            P("gx", "gy", None, None),
            P("gx", "gy", None, None, None),
            P(),
        ),
        out_specs=(P(None, "gx", "gy"), P("gx", "gy", None, None, None)),
        check_vma=False,
    )
```

```python
import functools

import jax
import jax.numpy as jnp
from jax import lax
from jax.experimental import pallas as pl
from jax.experimental.pallas import tpu as pltpu
from jax.sharding import PartitionSpec as P

MESH = pl.DeviceIdType.MESH
F32 = jnp.float32
BF16 = jnp.bfloat16

NU_COEF = 0.2
STEP_DT = 0.05
ATTEN_WATER = 0.06
ATTEN_CHL = 0.05
WARMING_SCALE = 0.5
GROWTH_TEMP = 0.063

LEVELS = 32
BLOCKS = 64
ROWS = 144
UNROLL = 4
LEVEL_STEP = 8
OUT_STEP = 8
OUT_CHUNK = 16
OUT_BUFS = 8
NT = (((1,), (1,)), ((), ()))
TN = (((0,), (0,)), ((), ()))


def iota(shape, dim):
    return lax.broadcasted_iota(jnp.int32, shape, dim)


def one_hot(mask):
    return jnp.where(mask, 1.0, 0.0).astype(BF16)


def swap_chunks(parts):
    lane = iota(parts[0].shape, 1)
    low = lane < 64
    even = (lane & 32) == 0
    a, b, c, d = parts
    a, c = jnp.where(low, a, pltpu.roll(c, 64, 1)), jnp.where(low, pltpu.roll(a, 64, 1), c)
    b, d = jnp.where(low, b, pltpu.roll(d, 64, 1)), jnp.where(low, pltpu.roll(b, 64, 1), d)
    a, b = jnp.where(even, a, pltpu.roll(b, 32, 1)), jnp.where(even, pltpu.roll(a, 96, 1), b)
    c, d = jnp.where(even, c, pltpu.roll(d, 32, 1)), jnp.where(even, pltpu.roll(c, 96, 1), d)
    return [a, b, c, d]


def exchange_kernel(
    gx_n,
    gy_n,
    t_hbm,
    amb_hbm,
    light_hbm,
    flag_hbm,
    tally_hbm,
    hold_hbm,
    rate_hbm,
    c_hbm,
    pre_ref,
    cnt_ref,
    shift_ref,
    therm_ref,
    t_ref,
    amb_ref,
    light_ref,
    flag_ref,
    tally_ref,
    hold_ref,
    rate_ref,
    c_ref,
    sel_ref,
    ut_ref,
    step_ref,
    pay_ref,
    recv_ref,
    hs_ref,
    hr_ref,
    tmp_ref,
    heat_ref,
    kap_ref,
    kup_ref,
    gv_ref,
    mix_ref,
    warm_ref,
    hxs_ref,
    hxr_ref,
    hys_ref,
    hyr_ref,
    ar_ref,
    ara_ref,
    arb_ref,
    in_sem,
    c_sem,
    halo_s,
    halo_r,
    fs_sem,
    fr_sem,
    own_sem,
    bs_sem,
    br_sem,
    as_sem,
    ar_sem,
    gs_sem,
    gr_sem,
):
    nz = gy_n // 4
    mx = lax.axis_index("gx")
    my = lax.axis_index("gy")
    mz = my // 4
    mq = my % 4

    def c_copy(z):
        return pltpu.make_async_copy(
            c_hbm.at[pl.ds(z * 32, 32)], c_ref.at[pl.ds(z * 32, 32)], c_sem.at[z]
        )

    loads = [
        pltpu.make_async_copy(src, dst, in_sem.at[n])
        for n, (src, dst) in enumerate(
            (
                (t_hbm, t_ref),
                (flag_hbm, flag_ref),
                (tally_hbm, tally_ref),
                (hold_hbm, hold_ref),
                (amb_hbm, amb_ref),
                (light_hbm, light_ref),
                (rate_hbm, rate_ref),
            )
        )
    ]
    for copy in loads:
        copy.start()

    bar = pltpu.get_barrier_semaphore()
    for d in range(1, gx_n):
        pl.semaphore_signal(
            bar, 1, device_id={"gx": (mx + d) % gx_n}, device_id_type=MESH
        )
    for d in range(1, gy_n):
        pl.semaphore_signal(
            bar, 1, device_id={"gy": (my + d) % gy_n}, device_id_type=MESH
        )

    for copy in loads:
        copy.wait()
    for q in range(nz):
        c_copy((mz - q + nz) % nz).start()

    dep = (flag_ref[...] * tally_ref[...]).astype(F32)
    hold = hold_ref[...].astype(F32)
    bi = iota((BLOCKS, BLOCKS), 0)
    bj = iota((BLOCKS, BLOCKS), 1)
    hold_b = jnp.broadcast_to(hold, (BLOCKS, BLOCKS))
    hold_c = jnp.sum(jnp.where(bi == bj, hold_b, 0.0), axis=1, keepdims=True)
    same = jnp.where((hold_c == hold_b) & (bi < bj), 1.0, 0.0)
    rank = jnp.sum(same, axis=0, keepdims=True)
    slot = hold * 8.0 + rank
    r8 = iota((8, BLOCKS), 0)
    pair = jnp.where(
        r8 == 0,
        jnp.broadcast_to(slot, (8, BLOCKS)),
        jnp.where(r8 == 1, jnp.broadcast_to(dep, (8, BLOCKS)), 0.0),
    ).astype(BF16)
    spread = one_hot(iota((BLOCKS, 512), 0) == (iota((BLOCKS, 512), 1) >> 3))
    lanes = jnp.dot(pair, spread, preferred_element_type=F32)
    slot_l = lanes[0:1]
    dep_l = lanes[1:2]
    lane8 = iota((8, 128), 1)
    dep_b = [
        jnp.broadcast_to(dep_l[:, 128 * bx : 128 * bx + 128], (8, 128)) for bx in range(4)
    ]
    cells = jnp.sum(dep, axis=1, keepdims=True) * 64.0

    hxs_ref[0, 0:32, :] = t_ref[:, 0, :]
    hxs_ref[1, 0:32, :] = t_ref[:, 31, :]
    hxs_ref[0, 32:40, :] = dep_b[0]
    hxs_ref[1, 32:40, :] = dep_b[3]

    zero8 = jnp.zeros((8, 128), F32)
    low4, high4 = [zero8] * 4, [zero8] * 4
    for k in range(LEVELS):
        for bx in range(4):
            part = t_ref[k, 8 * bx : 8 * bx + 8, :]
            place = 32 * bx + k
            low4[bx] = jnp.where(lane8 == place, pltpu.roll(part, place, 1), low4[bx])
            high4[bx] = jnp.where(
                lane8 == place, pltpu.roll(part, (place + 1) % 128, 1), high4[bx]
            )
    quarter = lane8 >> 5
    low = jnp.where(
        quarter < 2,
        jnp.where(quarter == 0, low4[0], low4[1]),
        jnp.where(quarter == 2, low4[2], low4[3]),
    )
    high = jnp.where(
        quarter < 2,
        jnp.where(quarter == 0, high4[0], high4[1]),
        jnp.where(quarter == 2, high4[2], high4[3]),
    )
    dlow, dhigh = zero8, zero8
    for bx in range(4):
        dlow = jnp.where(lane8 == 32 * bx, pltpu.roll(dep_b[bx], 32 * bx, 1), dlow)
        dhigh = jnp.where(lane8 == 32 * bx, pltpu.roll(dep_b[bx], 32 * bx + 1, 1), dhigh)
    hys_ref[0, 0:8, :] = low
    hys_ref[1, 0:8, :] = high
    hys_ref[0, 8:16, :] = dlow
    hys_ref[1, 8:16, :] = dhigh

    pl.semaphore_wait(bar, gx_n - 1 + gy_n - 1)

    def halo(side):
        step = gx_n - 1 if side == 0 else 1
        stepy = gy_n - 1 if side == 0 else 1
        return (
            pltpu.make_async_remote_copy(
                hxs_ref.at[side],
                hxr_ref.at[1 - side],
                halo_s.at[side],
                halo_r.at[side],
                device_id={"gx": (mx + step) % gx_n},
                device_id_type=MESH,
            ),
            pltpu.make_async_remote_copy(
                hys_ref.at[side],
                hyr_ref.at[1 - side],
                halo_s.at[2 + side],
                halo_r.at[2 + side],
                device_id={"gy": (my + stepy) % gy_n},
                device_id_type=MESH,
            ),
        )

    halos = halo(0) + halo(1)
    for copy in halos:
        copy.start()

    lane_n = iota((1, 512), 1)
    key_l = slot_l * 8.0 + (lane_n & 7).astype(F32)

    def build_sel(z, carry):
        m = iota((256, 1), 0) + z * 256
        key = ((m >> 6) << 6) | ((m & 7) << 3) | ((m >> 3) & 7)
        sel_ref[pl.ds(pl.multiple_of(z * 256, 256), 256), :] = one_hot(
            jnp.broadcast_to(key.astype(F32), (256, 512))
            == jnp.broadcast_to(key_l, (256, 512))
        )
        return carry

    lax.fori_loop(0, nz, build_sel, 0)

    def by_lanes(field):
        return jnp.concatenate([field[8 * bx : 8 * bx + 8] for bx in range(4)], axis=1)

    aux = jnp.concatenate(
        [
            by_lanes(light_ref[...].astype(F32)),
            by_lanes(amb_ref[...].astype(F32)),
            jnp.broadcast_to(dep_l, (8, 512)),
            jnp.zeros((8, 512), F32),
        ],
        axis=0,
    ).astype(BF16)
    er = iota((256, 32), 0)
    ef = iota((256, 32), 1)
    place = one_hot(ef == jnp.where(er < 128, er >> 3, 16))
    wide = jnp.dot(place, aux, preferred_element_type=F32)
    wide = jnp.where(
        (iota((256, 512), 0) & 7) == (iota((256, 512), 1) & 7), wide, 0.0
    ).astype(BF16)
    slots = 8 * gy_n
    sel_b = one_hot(
        iota((slots, 512), 0).astype(F32) == jnp.broadcast_to(slot_l, (slots, 512))
    )
    packed_aux = lax.dot_general(sel_b, wide, NT, preferred_element_type=F32)
    packed_aux = packed_aux.reshape(gy_n, 8, 256)
    pay_ref[:, 128:144, :] = jnp.concatenate(
        [packed_aux[:, :, :128], packed_aux[:, :, 128:]], axis=1
    ).astype(BF16)

    for copy in halos:
        copy.wait_recv()

    row = iota((32, 128), 0)
    lane = iota((32, 128), 1)
    on_low_x = jnp.where(mx > 0, 1.0, 0.0)
    on_high_x = jnp.where(mx < gx_n - 1, 1.0, 0.0)
    on_low_y = jnp.where(my > 0, 1.0, 0.0)
    on_high_y = jnp.where(my < gy_n - 1, 1.0, 0.0)

    def around(field, below_row, above_row, low_h, high_h):
        up = jnp.where(row == 0, below_row, pltpu.roll(field, 1, 0))
        down = jnp.where(row == 31, above_row, pltpu.roll(field, 31, 0))
        low_v = jnp.concatenate(
            [low_h] + [pltpu.roll(low_h, 128 - 32 * bx, 1) for bx in (1, 2, 3)], axis=0
        )
        high_v = jnp.concatenate(
            [pltpu.roll(high_h, 127 - 32 * bx, 1) for bx in range(4)], axis=0
        )
        west = jnp.where(lane == 0, low_v, pltpu.roll(field, 1, 1))
        east = jnp.where(lane == 127, high_v, pltpu.roll(field, 127, 1))
        return up, down, west, east

    dep2 = jnp.concatenate(dep_b, axis=0)
    dep_n = around(
        dep2,
        hxr_ref[0, 32:33, :] * on_low_x,
        hxr_ref[1, 32:33, :] * on_high_x,
        hyr_ref[0, 8:16, :] * on_low_y,
        hyr_ref[1, 8:16, :] * on_high_y,
    )

    def stencil(kk, carry):
        low_h, high_h = carry
        done = []
        for part in range(LEVEL_STEP):
            k = kk * LEVEL_STEP + part
            field = t_ref[k]
            near = around(
                field,
                hxr_ref[0, pl.ds(k, 1), :],
                hxr_ref[1, pl.ds(k, 1), :],
                low_h,
                high_h,
            )
            low_h = pltpu.roll(low_h, 127, 1)
            high_h = pltpu.roll(high_h, 127, 1)
            kf = k.astype(F32)
            total = jnp.where(dep_n[0] > kf, near[0] - field, 0.0)
            for d, n in zip(dep_n[1:], near[1:]):
                total = total + jnp.where(d > kf, n - field, 0.0)
            stepped = field + NU_COEF * jnp.where(dep2 > kf, total, 0.0)
            step_ref[k] = stepped
            done.append(stepped)
        size = 8 * LEVEL_STEP
        rows = pl.ds(pl.multiple_of(kk * size, size), size)
        for bx in range(4):
            ut_ref[rows, 128 * bx : 128 * bx + 128] = jnp.concatenate(
                [d[8 * bx : 8 * bx + 8] for d in done], axis=0
            ).astype(BF16)
        return low_h, high_h

    lax.fori_loop(
        0, LEVELS // LEVEL_STEP, stencil, (hyr_ref[0, 0:8, :], hyr_ref[1, 0:8, :]))

    def forward(other):
        return pltpu.make_async_remote_copy(
            pay_ref.at[other],
            recv_ref.at[my],
            fs_sem.at[other],
            fr_sem.at[my],
            device_id={"gy": other},
            device_id_type=MESH,
        )

    def arrival(other):
        return pltpu.make_async_remote_copy(
            pay_ref.at[other],
            recv_ref.at[other],
            fs_sem.at[other],
            fr_sem.at[other],
            device_id={"gy": other},
            device_id_type=MESH,
        )

    own = pltpu.make_async_copy(pay_ref.at[my], recv_ref.at[my], own_sem.at[0])
    for q in range(nz):
        z = (mz + q) % nz
        part = lax.dot_general(
            sel_ref[pl.ds(pl.multiple_of(z * 256, 256), 256), :],
            ut_ref[...],
            NT,
            preferred_element_type=F32,
        ).astype(BF16)
        part = part.reshape(4, 64, 256)
        pay_ref[pl.ds(z * 4, 4), 0:64, :] = part[:, :, :128]
        pay_ref[pl.ds(z * 4, 4), 64:128, :] = part[:, :, 128:]
        for d in range(4):
            if q == 0 and d == 0:
                own.start()
            else:
                forward(z * 4 + (mq + d) % 4).start()

    pi = iota((256, 256), 0)
    po = iota((256, 256), 1)
    to_columns = one_hot(po == (((pi & 31) << 3) | (pi >> 5)))
    from_columns = one_hot(pi == (((po & 31) << 3) | (po >> 5)))
    rates = jnp.concatenate([rate_ref[...]] * 32, axis=0)
    spread_r = (iota((8, 256), 1) & 7) == iota((8, 256), 0)
    rates_hi = rates.astype(BF16)
    rates_lo = (rates - rates_hi.astype(F32)).astype(BF16)
    spread_r = one_hot(spread_r)
    diagonal = (pi >> 3) == (po >> 3)
    mat_hi = jnp.where(
        diagonal, jnp.dot(rates_hi, spread_r, preferred_element_type=F32), 0.0
    ).astype(BF16)
    mat_lo = jnp.where(
        diagonal, jnp.dot(rates_lo, spread_r, preferred_element_type=F32), 0.0
    ).astype(BF16)
    upper = lane >= 64
    upper8 = lane8 >= 64
    sums = (zero8,) * 4

    def back(other):
        return pltpu.make_async_remote_copy(
            hs_ref.at[other],
            hr_ref.at[my],
            bs_sem.at[other],
            br_sem.at[my],
            device_id={"gy": other},
            device_id_type=MESH,
        )

    def back_arrival(other):
        return pltpu.make_async_remote_copy(
            hs_ref.at[other],
            hr_ref.at[other],
            bs_sem.at[other],
            br_sem.at[other],
            device_id={"gy": other},
            device_id_type=MESH,
        )

    own_back = pltpu.make_async_copy(hs_ref.at[my], hr_ref.at[my], own_sem.at[1])

    def gx_send(other):
        return pltpu.make_async_remote_copy(
            ar_ref.at[0],
            ara_ref.at[mx],
            as_sem.at[other],
            ar_sem.at[mx],
            device_id={"gx": other},
            device_id_type=MESH,
        )

    def gx_arrival(other):
        return pltpu.make_async_remote_copy(
            ar_ref.at[0],
            ara_ref.at[other],
            as_sem.at[other],
            ar_sem.at[other],
            device_id={"gx": other},
            device_id_type=MESH,
        )

    def gy_send(other):
        return pltpu.make_async_remote_copy(
            ar_ref.at[1],
            arb_ref.at[my],
            gs_sem.at[other],
            gr_sem.at[my],
            device_id={"gy": other},
            device_id_type=MESH,
        )

    def gy_arrival(other):
        return pltpu.make_async_remote_copy(
            ar_ref.at[1],
            arb_ref.at[other],
            gs_sem.at[other],
            gr_sem.at[other],
            device_id={"gy": other},
            device_id_type=MESH,
        )

    def gx_sums(sums):
        ar_ref[0, 0:8, :] = (sums[0] + sums[1]) + (sums[2] + sums[3])
        ar_ref[0, 8:16, :] = jnp.broadcast_to(cells, (8, 128))
        for d in range(1, gx_n):
            gx_send((mx + d) % gx_n).start()
        ara_ref[mx] = ar_ref[0]

    for q in range(nz):
        z = (mz - q + nz) % nz
        s0 = z * 32
        for d in range(4):
            if q == 0 and d == 0:
                own.wait()
            else:
                arrival(z * 4 + (mq - d + 4) % 4).wait_recv()
        c_copy(z).wait()
        blk = recv_ref[pl.ds(z * 4, 4), :, :].astype(F32)
        rows = []
        for h in range(2):
            quads = []
            for yh in range(2):
                quads.append(
                    swap_chunks(
                        [
                            blk[:, h * 64 + y * 8 : h * 64 + y * 8 + 8, :].reshape(32, 128)
                            for y in range(yh * 4, yh * 4 + 4)
                        ]
                    )
                )
            for g in range(4):
                rows.append(jnp.concatenate([quads[0][g], quads[1][g]], axis=1))
        cols = jnp.dot(
            jnp.concatenate(rows, axis=0).astype(BF16),
            to_columns,
            preferred_element_type=F32,
        )
        for g in range(8):
            tmp_ref[:, g * 256 : g * 256 + 256] = cols[g * 32 : g * 32 + 32]

        la = blk[:, 128:136, :].reshape(32, 128)
        cnt = blk[:, 136:144, :].reshape(32, 128)
        cnt_ref[pl.ds(s0, 32), :] = cnt
        la_r = pltpu.roll(la, 64, 1)
        light = jnp.where(upper, la_r, la)
        amb = jnp.where(upper, la, la_r)
        level = jnp.where(upper, 1.0, 0.0)
        run = jnp.zeros((32, 128), F32)
        prev = light
        kap_prev = jnp.zeros((32, 128), F32)
        t_next = tmp_ref[:, 0:128]
        tr_next = pltpu.roll(t_next, 64, 1)
        for i in range(16):
            at = slice(128 * i, 128 * i + 128)
            t_i, tr_i = t_next, tr_next
            if i < 15:
                t_next = tmp_ref[:, 128 * i + 128 : 128 * i + 256]
                tr_next = pltpu.roll(t_next, 64, 1)
                t_below = jnp.where(upper, tr_next, tr_i)
            else:
                t_below = jnp.where(upper, t_i, tr_i)
            atten = ATTEN_WATER + ATTEN_CHL * c_ref[pl.ds(s0, 32), 0, at]
            atten_r = pltpu.roll(atten, 64, 1)
            both = atten + atten_r
            cum = run + jnp.where(upper, both, atten)
            run = run + both
            bottom = light * jnp.exp(-cum)
            bottom_r = pltpu.roll(bottom, 64, 1)
            top = jnp.where(upper, bottom_r, prev)
            prev = bottom_r
            wet = cnt - 2.0 * i > level
            heat_ref[:, at] = jnp.where(wet, top - bottom, 0.0)
            growth = jnp.exp(GROWTH_TEMP * t_i) * top / (top + 1.0)
            gv_ref[i, 0:32] = jnp.where(wet, STEP_DT * growth, 0.0)
            kap = amb * (1.0 + 0.5 * jnp.tanh(t_i - t_below))
            kap = jnp.where(cnt - (2.0 * i + 1.0) > level, STEP_DT * kap, 0.0)
            kap_r = pltpu.roll(kap, 64, 1)
            kap_ref[i, 0:32] = kap
            kup_ref[i, 0:32] = jnp.where(upper, kap_r, kap_prev)
            kap_prev = kap_r

        heat = jnp.concatenate(
            [heat_ref[:, g * 256 : g * 256 + 256] for g in range(8)], axis=0
        ).astype(BF16)
        back_cols = jnp.dot(heat, from_columns, preferred_element_type=F32)
        for h in range(2):
            quads = [
                swap_chunks(
                    [
                        back_cols[
                            (h * 4 + g) * 32 : (h * 4 + g) * 32 + 32, yh * 128 : yh * 128 + 128
                        ]
                        for g in range(4)
                    ]
                )
                for yh in range(2)
            ]
            flat = [p.reshape(4, 8, 128) for p in quads[0] + quads[1]]
            for y in range(0, 8, 2):
                hs_ref[pl.ds(z * 4, 4), h * 64 + y * 8 : h * 64 + y * 8 + 16, :] = (
                    jnp.concatenate([flat[y], flat[y + 1]], axis=1).astype(BF16)
                )
        for d in range(4):
            if q == 0 and d == 0:
                own_back.start()
            else:
                back(z * 4 + (mq - d + 4) % 4).start()

        for g in range(8):
            at = slice(256 * g, 256 * g + 256)
            c_b = c_ref[pl.ds(s0, 32), :, at].reshape(256, 256).astype(BF16)
            mix_ref[:, at] = jnp.dot(mat_hi, c_b, preferred_element_type=F32) + jnp.dot(
                mat_lo, c_b, preferred_element_type=F32
            )

        def row_of(ref, i, s):
            return ref[i, pl.ds(s, 8, stride=0), :]

        def mix_of(i, s):
            return mix_ref[
                pl.ds(pl.multiple_of(s * 8, 8), 8), 128 * i : 128 * i + 128
            ]

        def grow(step, acc):
            acc = list(acc)
            for u in range(UNROLL):
                s = step * UNROLL + u
                for i in range(16):
                    acc[i % 4] = acc[i % 4] + row_of(gv_ref, i, s) * mix_of(i, s)
            return tuple(acc)

        def tracers(counted, step, acc):
            acc = list(acc)
            for u in range(UNROLL):
                s = step * UNROLL + u
                c_next = c_ref[s0 + s, :, 0:128]
                cr_next = pltpu.roll(c_next, 64, 1)
                cr_i = cr_next
                for i in range(16):
                    at = slice(128 * i, 128 * i + 128)
                    cr_prev = cr_i
                    c_i, cr_i = c_next, cr_next
                    if i < 15:
                        c_next = c_ref[s0 + s, :, 128 * i + 128 : 128 * i + 256]
                        cr_next = pltpu.roll(c_next, 64, 1)
                    below = jnp.where(upper8, cr_next, cr_i)
                    above = jnp.where(upper8, cr_i, cr_prev)
                    grown = row_of(gv_ref, i, s) * mix_of(i, s)
                    if counted:
                        acc[i % 4] = acc[i % 4] + grown
                    pre_ref[s0 + s, :, at] = (c_i + row_of(kap_ref, i, s) * (below - c_i)) + (
                        row_of(kup_ref, i, s) * (above - c_i) + grown
                    )
            return tuple(acc)

        last = q == nz - 1
        steps = 32 // UNROLL
        if last:
            sums = lax.fori_loop(0, steps, grow, sums)
            gx_sums(sums)
        sums = lax.fori_loop(0, steps, functools.partial(tracers, not last), sums)

    for d in range(1, gx_n):
        gx_arrival((mx + d) % gx_n).wait_recv()
    ar_ref[1] = jnp.sum(ara_ref[...], axis=0)
    for d in range(1, gy_n):
        gy_send((my + d) % gy_n).start()
    arb_ref[my] = ar_ref[1]

    for q in range(nz):
        z = (mz + q) % nz
        for d in range(4):
            if q == 0 and d == 0:
                own_back.wait()
            else:
                back_arrival(z * 4 + (mq + d) % 4).wait_recv()
        got = hr_ref[pl.ds(z * 4, 4), :, :]
        sel = sel_ref[pl.ds(pl.multiple_of(z * 256, 256), 256), :]
        for h in range(2):
            lhs = got[:, h * 64 : h * 64 + 64, :].reshape(256, 128)
            warm = lax.dot_general(lhs, sel, TN, preferred_element_type=F32)
            rows_h = slice(128 * h, 128 * h + 128)
            if q == 0:
                warm_ref[rows_h, :] = warm
            else:
                warm_ref[rows_h, :] = warm_ref[rows_h, :] + warm

    def finish(k, carry):
        part = warm_ref[pl.ds(pl.multiple_of(k * 8, 8), 8), :]
        for bx in range(4):
            therm_ref[k, 8 * bx : 8 * bx + 8, :] = (
                step_ref[k, 8 * bx : 8 * bx + 8, :]
                + WARMING_SCALE * part[:, 128 * bx : 128 * bx + 128]
            )
        return carry

    lax.fori_loop(0, LEVELS, finish, 0)

    for d in range(1, gy_n):
        gy_arrival((my + d) % gy_n).wait_recv()
    total = jnp.sum(arb_ref[...], axis=0)
    grown = jnp.sum(total[0:8], axis=1, keepdims=True)
    shift_ref[...] = -(jnp.broadcast_to(grown, (8, 128)) / jnp.maximum(total[8:16], 1.0))

    for copy in halos:
        copy.wait_send()
    for d in range(1, gy_n):
        forward((my + d) % gy_n).wait_send()
        back((my + d) % gy_n).wait_send()
        gy_send((my + d) % gy_n).wait_send()
    for d in range(1, gx_n):
        gx_send((mx + d) % gx_n).wait_send()


def finish_kernel(pre_ref, cnt_ref, shift_ref, therm_ref, out_ref, thout_ref, buf_ref, sem):
    level = jnp.where(iota((8, 128), 1) >= 64, 1.0, 0.0)
    n = pre_ref.shape[0] // OUT_CHUNK
    thermal = pltpu.make_async_copy(therm_ref, thout_ref, sem.at[OUT_BUFS])
    thermal.start()
    shift = shift_ref[...]

    def out_copy(c):
        return pltpu.make_async_copy(
            buf_ref.at[c % OUT_BUFS],
            out_ref.at[pl.ds(c * OUT_CHUNK, OUT_CHUNK)],
            sem.at[c % OUT_BUFS],
        )

    for c in range(n):
        if c >= OUT_BUFS:
            out_copy(c - OUT_BUFS).wait()

        def some(step, carry):
            for u in range(OUT_STEP):
                s = step * OUT_STEP + u
                wet = cnt_ref[pl.ds(c * OUT_CHUNK + s, 8, stride=0), :] - level
                for i in range(16):
                    at = slice(128 * i, 128 * i + 128)
                    buf_ref[c % OUT_BUFS, s, :, at] = pre_ref[
                        c * OUT_CHUNK + s, :, at
                    ] + jnp.where(wet > 2.0 * i, shift, 0.0)
            return carry

        lax.fori_loop(0, OUT_CHUNK // OUT_STEP, some, 0)
        out_copy(c).start()
    for c in range(max(n - OUT_BUFS, 0), n):
        out_copy(c).wait()
    thermal.wait()


def solution(mesh):
    gx_n = mesh.shape["gx"]
    gy_n = mesh.shape["gy"]
    slots = 8 * gy_n

    def on_device(thermal, amb, light, flags, tally, hold, solutes, rates):
        dma = pltpu.SemaphoreType.DMA
        vmem = pl.BlockSpec(memory_space=pltpu.VMEM)
        hbm = pl.BlockSpec(memory_space=pltpu.HBM)
        tracers = solutes.reshape(slots, 8, 2048)
        pre, cnt, shift, therm = pl.pallas_call(
            functools.partial(exchange_kernel, gx_n, gy_n),
            out_shape=[
                pltpu.VMEM((slots, 8, 2048), F32),
                pltpu.VMEM((slots + 8, 128), F32),
                pltpu.VMEM((8, 128), F32),
                pltpu.VMEM((32, 32, 128), F32),
            ],
            in_specs=[hbm] * 8,
            out_specs=[vmem] * 4,
            scratch_shapes=[
                pltpu.VMEM((32, 32, 128), F32),
                pltpu.VMEM((32, 128), BF16),
                pltpu.VMEM((32, 128), BF16),
                pltpu.VMEM((1, BLOCKS), jnp.int32),
                pltpu.VMEM((1, BLOCKS), jnp.int32),
                pltpu.VMEM((1, BLOCKS), jnp.int32),
                pltpu.VMEM((8, 8), F32),
                pltpu.VMEM((slots, 8, 2048), F32),
                pltpu.VMEM((64 * gy_n, 512), BF16),
                pltpu.VMEM((256, 512), BF16),
                pltpu.VMEM((32, 32, 128), F32),
                pltpu.VMEM((gy_n, ROWS, 128), BF16),
                pltpu.VMEM((gy_n, ROWS, 128), BF16),
                pltpu.VMEM((gy_n, 128, 128), BF16),
                pltpu.VMEM((gy_n, 128, 128), BF16),
                pltpu.VMEM((32, 2048), F32),
                pltpu.VMEM((32, 2048), F32),
                pltpu.VMEM((16, 40, 128), F32),
                pltpu.VMEM((16, 40, 128), F32),
                pltpu.VMEM((16, 40, 128), F32),
                pltpu.VMEM((256, 2048), F32),
                pltpu.VMEM((256, 512), F32),
                pltpu.VMEM((2, 40, 128), F32),
                pltpu.VMEM((2, 40, 128), F32),
                pltpu.VMEM((2, 16, 128), F32),
                pltpu.VMEM((2, 16, 128), F32),
                pltpu.VMEM((2, 16, 128), F32),
                pltpu.VMEM((gx_n, 16, 128), F32),
                pltpu.VMEM((gy_n, 16, 128), F32),
                dma((7,)),
                dma((gy_n // 4,)),
                dma((4,)),
                dma((4,)),
                dma((gy_n,)),
                dma((gy_n,)),
                dma((2,)),
                dma((gy_n,)),
                dma((gy_n,)),
                dma((gx_n,)),
                dma((gx_n,)),
                dma((gy_n,)),
                dma((gy_n,)),
            ],
            compiler_params=pltpu.CompilerParams(
                collective_id=0, has_side_effects=True, vmem_limit_bytes=40 * 1024 * 1024
            ),
            name="exchange",
        )(
            *(
                pltpu.with_memory_space_constraint(a, pltpu.HBM)
                for a in (
                    thermal,
                    amb,
                    light,
                    flags.reshape(1, BLOCKS),
                    tally.reshape(1, BLOCKS),
                    hold.reshape(1, BLOCKS),
                    rates,
                    tracers,
                )
            )
        )
        out, therm_out = pl.pallas_call(
            finish_kernel,
            out_shape=[
                jax.ShapeDtypeStruct((slots, 8, 2048), F32),
                jax.ShapeDtypeStruct((32, 32, 128), F32),
            ],
            in_specs=[vmem] * 4,
            out_specs=[hbm] * 2,
            scratch_shapes=[
                pltpu.VMEM((OUT_BUFS, OUT_CHUNK, 8, 2048), F32),
                dma((OUT_BUFS + 1,)),
            ],
            compiler_params=pltpu.CompilerParams(vmem_limit_bytes=16 * 1024 * 1024),
            name="finish",
        )(pre, cnt, shift, therm)
        return therm_out, out.reshape(solutes.shape)

    return jax.shard_map(
        on_device,
        mesh=mesh,
        in_specs=(
            P(None, "gx", "gy"),
            P("gx", "gy"),
            P("gx", "gy"),
            P("gx", "gy", None),
            P("gx", "gy", None),
            P("gx", "gy", None, None),
            P("gx", "gy", None, None, None),
            P(),
        ),
        out_specs=(P(None, "gx", "gy"), P("gx", "gy", None, None, None)),
        check_vma=False,
    )
```

```python
import functools

import jax
import jax.numpy as jnp
from jax import lax
from jax.experimental import pallas as pl
from jax.experimental.pallas import tpu as pltpu
from jax.sharding import PartitionSpec as P

MESH = pl.DeviceIdType.MESH
F32 = jnp.float32
BF16 = jnp.bfloat16

NU_COEF = 0.2
STEP_DT = 0.05
ATTEN_WATER = 0.06
ATTEN_CHL = 0.05
WARMING_SCALE = 0.5
GROWTH_TEMP = 0.063

LEVELS = 32
BLOCKS = 64
UNROLL = 4
LEVEL_STEP = 8
OUT_STEP = 8
OUT_CHUNK = 16
OUT_BUFS = 8
NT = (((1,), (1,)), ((), ()))
TN = (((0,), (0,)), ((), ()))


def iota(shape, dim):
    return lax.broadcasted_iota(jnp.int32, shape, dim)


def one_hot(mask):
    return jnp.where(mask, 1.0, 0.0).astype(BF16)


def swap_chunks(parts):
    lane = iota(parts[0].shape, 1)
    low = lane < 64
    even = (lane & 32) == 0
    a, b, c, d = parts
    a, c = jnp.where(low, a, pltpu.roll(c, 64, 1)), jnp.where(low, pltpu.roll(a, 64, 1), c)
    b, d = jnp.where(low, b, pltpu.roll(d, 64, 1)), jnp.where(low, pltpu.roll(b, 64, 1), d)
    a, b = jnp.where(even, a, pltpu.roll(b, 32, 1)), jnp.where(even, pltpu.roll(a, 96, 1), b)
    c, d = jnp.where(even, c, pltpu.roll(d, 32, 1)), jnp.where(even, pltpu.roll(c, 96, 1), d)
    return [a, b, c, d]


def exchange_kernel(
    gx_n,
    gy_n,
    t_hbm,
    amb_hbm,
    light_hbm,
    flag_hbm,
    tally_hbm,
    hold_hbm,
    rate_hbm,
    c_hbm,
    pre_ref,
    cnt_ref,
    shift_ref,
    therm_ref,
    t_ref,
    amb_ref,
    light_ref,
    flag_ref,
    tally_ref,
    hold_ref,
    rate_ref,
    c_ref,
    sel_ref,
    ut_ref,
    step_ref,
    pay_ref,
    recv_ref,
    ax_ref,
    axr_ref,
    top_ref,
    hs_ref,
    hr_ref,
    tmp_ref,
    heat_ref,
    kap_ref,
    kup_ref,
    gv_ref,
    mix_ref,
    warm_ref,
    hxs_ref,
    hxr_ref,
    hys_ref,
    hyr_ref,
    ar_ref,
    ara_ref,
    arb_ref,
    in_sem,
    c_sem,
    halo_s,
    halo_r,
    xs_sem,
    xr_sem,
    fs_sem,
    fr_sem,
    own_sem,
    bs_sem,
    br_sem,
    as_sem,
    ar_sem,
    gs_sem,
    gr_sem,
):
    nz = gy_n // 4
    mx = lax.axis_index("gx")
    my = lax.axis_index("gy")
    mz = my // 4
    mq = my % 4

    def c_copy(z):
        return pltpu.make_async_copy(
            c_hbm.at[pl.ds(z * 32, 32)], c_ref.at[pl.ds(z * 32, 32)], c_sem.at[z]
        )

    loads = [
        pltpu.make_async_copy(src, dst, in_sem.at[n])
        for n, (src, dst) in enumerate(
            (
                (t_hbm, t_ref),
                (flag_hbm, flag_ref),
                (tally_hbm, tally_ref),
                (hold_hbm, hold_ref),
                (amb_hbm, amb_ref),
                (light_hbm, light_ref),
                (rate_hbm, rate_ref),
            )
        )
    ]
    for copy in loads:
        copy.start()

    bar = pltpu.get_barrier_semaphore()
    for d in range(1, gx_n):
        pl.semaphore_signal(
            bar, 1, device_id={"gx": (mx + d) % gx_n}, device_id_type=MESH
        )
    for d in range(1, gy_n):
        pl.semaphore_signal(
            bar, 1, device_id={"gy": (my + d) % gy_n}, device_id_type=MESH
        )

    for copy in loads:
        copy.wait()
    for q in range(nz):
        c_copy((mz - q + nz) % nz).start()

    dep = (flag_ref[...] * tally_ref[...]).astype(F32)
    hold = hold_ref[...].astype(F32)
    bi = iota((BLOCKS, BLOCKS), 0)
    bj = iota((BLOCKS, BLOCKS), 1)
    hold_b = jnp.broadcast_to(hold, (BLOCKS, BLOCKS))
    hold_c = jnp.sum(jnp.where(bi == bj, hold_b, 0.0), axis=1, keepdims=True)
    same = jnp.where((hold_c == hold_b) & (bi < bj), 1.0, 0.0)
    rank = jnp.sum(same, axis=0, keepdims=True)
    slot = hold * 8.0 + rank
    r8 = iota((8, BLOCKS), 0)
    pair = jnp.where(
        r8 == 0,
        jnp.broadcast_to(slot, (8, BLOCKS)),
        jnp.where(r8 == 1, jnp.broadcast_to(dep, (8, BLOCKS)), 0.0),
    ).astype(BF16)
    spread = one_hot(iota((BLOCKS, 512), 0) == (iota((BLOCKS, 512), 1) >> 3))
    lanes = jnp.dot(pair, spread, preferred_element_type=F32)
    slot_l = lanes[0:1]
    dep_l = lanes[1:2]
    lane8 = iota((8, 128), 1)
    dep_b = [
        jnp.broadcast_to(dep_l[:, 128 * bx : 128 * bx + 128], (8, 128)) for bx in range(4)
    ]
    cells = jnp.sum(dep, axis=1, keepdims=True) * 64.0

    hxs_ref[0, 0:32, :] = t_ref[:, 0, :]
    hxs_ref[1, 0:32, :] = t_ref[:, 31, :]
    hxs_ref[0, 32:40, :] = dep_b[0]
    hxs_ref[1, 32:40, :] = dep_b[3]

    zero8 = jnp.zeros((8, 128), F32)
    low4, high4 = [zero8] * 4, [zero8] * 4
    for k in range(LEVELS):
        for bx in range(4):
            part = t_ref[k, 8 * bx : 8 * bx + 8, :]
            place = 32 * bx + k
            low4[bx] = jnp.where(lane8 == place, pltpu.roll(part, place, 1), low4[bx])
            high4[bx] = jnp.where(
                lane8 == place, pltpu.roll(part, (place + 1) % 128, 1), high4[bx]
            )
    quarter = lane8 >> 5
    low = jnp.where(
        quarter < 2,
        jnp.where(quarter == 0, low4[0], low4[1]),
        jnp.where(quarter == 2, low4[2], low4[3]),
    )
    high = jnp.where(
        quarter < 2,
        jnp.where(quarter == 0, high4[0], high4[1]),
        jnp.where(quarter == 2, high4[2], high4[3]),
    )
    dlow, dhigh = zero8, zero8
    for bx in range(4):
        dlow = jnp.where(lane8 == 32 * bx, pltpu.roll(dep_b[bx], 32 * bx, 1), dlow)
        dhigh = jnp.where(lane8 == 32 * bx, pltpu.roll(dep_b[bx], 32 * bx + 1, 1), dhigh)
    hys_ref[0, 0:8, :] = low
    hys_ref[1, 0:8, :] = high
    hys_ref[0, 8:16, :] = dlow
    hys_ref[1, 8:16, :] = dhigh

    pl.semaphore_wait(bar, gx_n - 1 + gy_n - 1)

    def halo(side):
        step = gx_n - 1 if side == 0 else 1
        stepy = gy_n - 1 if side == 0 else 1
        return (
            pltpu.make_async_remote_copy(
                hxs_ref.at[side],
                hxr_ref.at[1 - side],
                halo_s.at[side],
                halo_r.at[side],
                device_id={"gx": (mx + step) % gx_n},
                device_id_type=MESH,
            ),
            pltpu.make_async_remote_copy(
                hys_ref.at[side],
                hyr_ref.at[1 - side],
                halo_s.at[2 + side],
                halo_r.at[2 + side],
                device_id={"gy": (my + stepy) % gy_n},
                device_id_type=MESH,
            ),
        )

    halos = halo(0) + halo(1)
    for copy in halos:
        copy.start()

    def by_lanes(field):
        return jnp.concatenate([field[8 * bx : 8 * bx + 8] for bx in range(4)], axis=1)

    aux = jnp.concatenate(
        [
            by_lanes(light_ref[...].astype(F32)),
            by_lanes(amb_ref[...].astype(F32)),
            jnp.broadcast_to(dep_l, (8, 512)),
            jnp.zeros((8, 512), F32),
        ],
        axis=0,
    ).astype(BF16)
    er = iota((256, 32), 0)
    ef = iota((256, 32), 1)
    place = one_hot(ef == jnp.where(er < 128, er >> 3, 16))
    wide = jnp.dot(place, aux, preferred_element_type=F32)
    wide = jnp.where(
        (iota((256, 512), 0) & 7) == (iota((256, 512), 1) & 7), wide, 0.0
    ).astype(BF16)
    slots = 8 * gy_n
    sel_b = one_hot(
        iota((slots, 512), 0).astype(F32) == jnp.broadcast_to(slot_l, (slots, 512))
    )
    packed_aux = lax.dot_general(sel_b, wide, NT, preferred_element_type=F32)
    packed_aux = packed_aux.reshape(gy_n, 8, 256)
    ax_ref[...] = jnp.concatenate(
        [packed_aux[:, :, :128], packed_aux[:, :, 128:]], axis=1
    ).astype(BF16)

    def aux_send(other):
        return pltpu.make_async_remote_copy(
            ax_ref.at[other],
            axr_ref.at[my],
            xs_sem.at[other],
            xr_sem.at[my],
            device_id={"gy": other},
            device_id_type=MESH,
        )

    def aux_arrival(other):
        return pltpu.make_async_remote_copy(
            ax_ref.at[other],
            axr_ref.at[other],
            xs_sem.at[other],
            xr_sem.at[other],
            device_id={"gy": other},
            device_id_type=MESH,
        )

    own_aux = pltpu.make_async_copy(ax_ref.at[my], axr_ref.at[my], own_sem.at[2])
    own_aux.start()
    for d in range(1, gy_n):
        aux_send((my + d) % gy_n).start()

    lane_n = iota((1, 512), 1)
    key_l = slot_l * 8.0 + (lane_n & 7).astype(F32)

    def build_sel(z, carry):
        m = iota((256, 1), 0) + z * 256
        key = ((m >> 6) << 6) | ((m & 7) << 3) | ((m >> 3) & 7)
        sel_ref[pl.ds(pl.multiple_of(z * 256, 256), 256), :] = one_hot(
            jnp.broadcast_to(key.astype(F32), (256, 512))
            == jnp.broadcast_to(key_l, (256, 512))
        )
        return carry

    lax.fori_loop(0, nz, build_sel, 0)

    for copy in halos:
        copy.wait_recv()

    row = iota((32, 128), 0)
    lane = iota((32, 128), 1)
    on_low_x = jnp.where(mx > 0, 1.0, 0.0)
    on_high_x = jnp.where(mx < gx_n - 1, 1.0, 0.0)
    on_low_y = jnp.where(my > 0, 1.0, 0.0)
    on_high_y = jnp.where(my < gy_n - 1, 1.0, 0.0)

    def around(field, below_row, above_row, low_h, high_h):
        up = jnp.where(row == 0, below_row, pltpu.roll(field, 1, 0))
        down = jnp.where(row == 31, above_row, pltpu.roll(field, 31, 0))
        low_v = jnp.concatenate(
            [low_h] + [pltpu.roll(low_h, 128 - 32 * bx, 1) for bx in (1, 2, 3)], axis=0
        )
        high_v = jnp.concatenate(
            [pltpu.roll(high_h, 127 - 32 * bx, 1) for bx in range(4)], axis=0
        )
        west = jnp.where(lane == 0, low_v, pltpu.roll(field, 1, 1))
        east = jnp.where(lane == 127, high_v, pltpu.roll(field, 127, 1))
        return up, down, west, east

    dep2 = jnp.concatenate(dep_b, axis=0)
    dep_n = around(
        dep2,
        hxr_ref[0, 32:33, :] * on_low_x,
        hxr_ref[1, 32:33, :] * on_high_x,
        hyr_ref[0, 8:16, :] * on_low_y,
        hyr_ref[1, 8:16, :] * on_high_y,
    )

    def stencil(kk, carry):
        low_h, high_h = carry
        done = []
        for part in range(LEVEL_STEP):
            k = kk * LEVEL_STEP + part
            field = t_ref[k]
            near = around(
                field,
                hxr_ref[0, pl.ds(k, 1), :],
                hxr_ref[1, pl.ds(k, 1), :],
                low_h,
                high_h,
            )
            low_h = pltpu.roll(low_h, 127, 1)
            high_h = pltpu.roll(high_h, 127, 1)
            kf = k.astype(F32)
            total = jnp.where(dep_n[0] > kf, near[0] - field, 0.0)
            for d, n in zip(dep_n[1:], near[1:]):
                total = total + jnp.where(d > kf, n - field, 0.0)
            stepped = field + NU_COEF * jnp.where(dep2 > kf, total, 0.0)
            step_ref[k] = stepped
            done.append(stepped)
        size = 8 * LEVEL_STEP
        rows = pl.ds(pl.multiple_of(kk * size, size), size)
        for bx in range(4):
            ut_ref[rows, 128 * bx : 128 * bx + 128] = jnp.concatenate(
                [d[8 * bx : 8 * bx + 8] for d in done], axis=0
            ).astype(BF16)
        return low_h, high_h

    lax.fori_loop(
        0, LEVELS // LEVEL_STEP, stencil, (hyr_ref[0, 0:8, :], hyr_ref[1, 0:8, :]))

    def forward(other):
        return pltpu.make_async_remote_copy(
            pay_ref.at[other],
            recv_ref.at[my],
            fs_sem.at[other],
            fr_sem.at[my],
            device_id={"gy": other},
            device_id_type=MESH,
        )

    def arrival(other):
        return pltpu.make_async_remote_copy(
            pay_ref.at[other],
            recv_ref.at[other],
            fs_sem.at[other],
            fr_sem.at[other],
            device_id={"gy": other},
            device_id_type=MESH,
        )

    own = pltpu.make_async_copy(pay_ref.at[my], recv_ref.at[my], own_sem.at[0])
    for q in range(nz):
        z = (mz + q) % nz
        part = lax.dot_general(
            sel_ref[pl.ds(pl.multiple_of(z * 256, 256), 256), :],
            ut_ref[...],
            NT,
            preferred_element_type=F32,
        ).astype(BF16)
        part = part.reshape(4, 64, 256)
        pay_ref[pl.ds(z * 4, 4), 0:64, :] = part[:, :, :128]
        pay_ref[pl.ds(z * 4, 4), 64:128, :] = part[:, :, 128:]
        for d in range(4):
            if q == 0 and d == 0:
                own.start()
            else:
                forward(z * 4 + (mq + d) % 4).start()

    pi = iota((256, 256), 0)
    po = iota((256, 256), 1)
    to_columns = one_hot(po == (((pi & 31) << 3) | (pi >> 5)))
    from_columns = one_hot(pi == (((po & 31) << 3) | (po >> 5)))
    rates = jnp.concatenate([rate_ref[...]] * 32, axis=0)
    spread_r = (iota((8, 256), 1) & 7) == iota((8, 256), 0)
    rates_hi = rates.astype(BF16)
    rates_lo = (rates - rates_hi.astype(F32)).astype(BF16)
    spread_r = one_hot(spread_r)
    diagonal = (pi >> 3) == (po >> 3)
    mat_hi = jnp.where(
        diagonal, jnp.dot(rates_hi, spread_r, preferred_element_type=F32), 0.0
    ).astype(BF16)
    mat_lo = jnp.where(
        diagonal, jnp.dot(rates_lo, spread_r, preferred_element_type=F32), 0.0
    ).astype(BF16)
    upper = lane >= 64
    upper8 = lane8 >= 64
    level = jnp.where(upper, 1.0, 0.0)
    sums = (zero8,) * 4

    def back(other):
        return pltpu.make_async_remote_copy(
            hs_ref.at[other],
            hr_ref.at[my],
            bs_sem.at[other],
            br_sem.at[my],
            device_id={"gy": other},
            device_id_type=MESH,
        )

    def back_arrival(other):
        return pltpu.make_async_remote_copy(
            hs_ref.at[other],
            hr_ref.at[other],
            bs_sem.at[other],
            br_sem.at[other],
            device_id={"gy": other},
            device_id_type=MESH,
        )

    own_back = pltpu.make_async_copy(hs_ref.at[my], hr_ref.at[my], own_sem.at[1])

    def gx_send(other):
        return pltpu.make_async_remote_copy(
            ar_ref.at[0],
            ara_ref.at[mx],
            as_sem.at[other],
            ar_sem.at[mx],
            device_id={"gx": other},
            device_id_type=MESH,
        )

    def gx_arrival(other):
        return pltpu.make_async_remote_copy(
            ar_ref.at[0],
            ara_ref.at[other],
            as_sem.at[other],
            ar_sem.at[other],
            device_id={"gx": other},
            device_id_type=MESH,
        )

    def gy_send(other):
        return pltpu.make_async_remote_copy(
            ar_ref.at[1],
            arb_ref.at[my],
            gs_sem.at[other],
            gr_sem.at[my],
            device_id={"gy": other},
            device_id_type=MESH,
        )

    def gy_arrival(other):
        return pltpu.make_async_remote_copy(
            ar_ref.at[1],
            arb_ref.at[other],
            gs_sem.at[other],
            gr_sem.at[other],
            device_id={"gy": other},
            device_id_type=MESH,
        )

    def gx_sums(sums):
        ar_ref[0, 0:8, :] = (sums[0] + sums[1]) + (sums[2] + sums[3])
        ar_ref[0, 8:16, :] = jnp.broadcast_to(cells, (8, 128))
        for d in range(1, gx_n):
            gx_send((mx + d) % gx_n).start()
        ara_ref[mx] = ar_ref[0]

    def row_of(ref, i, s):
        return ref[i, pl.ds(s, 8, stride=0), :]

    def mix_of(i, s):
        return mix_ref[pl.ds(pl.multiple_of(s * 8, 8), 8), 128 * i : 128 * i + 128]

    for q in range(nz):
        z = (mz - q + nz) % nz
        s0 = z * 32
        for d in range(4):
            if q == 0 and d == 0:
                own_aux.wait()
            else:
                aux_arrival(z * 4 + (mq - d + 4) % 4).wait_recv()
        c_copy(z).wait()
        got = axr_ref[pl.ds(z * 4, 4), :, :].astype(F32)
        la = got[:, 0:8, :].reshape(32, 128)
        cnt = got[:, 8:16, :].reshape(32, 128)
        cnt_ref[pl.ds(s0, 32), :] = cnt
        light = jnp.where(upper, pltpu.roll(la, 64, 1), la)
        run = jnp.zeros((32, 128), F32)
        prev = light
        wet = cnt - level
        for i in range(16):
            at = slice(128 * i, 128 * i + 128)
            atten = ATTEN_WATER + ATTEN_CHL * c_ref[pl.ds(s0, 32), 0, at]
            both = atten + pltpu.roll(atten, 64, 1)
            cum = run + jnp.where(upper, both, atten)
            run = run + both
            bottom = light * jnp.exp(-cum)
            bottom_r = pltpu.roll(bottom, 64, 1)
            top = jnp.where(upper, bottom_r, prev)
            prev = bottom_r
            top_ref[i, pl.ds(s0, 32), :] = top
            heat_ref[:, at] = jnp.where(wet > 2.0 * i, top - bottom, 0.0)
        heat = jnp.concatenate(
            [heat_ref[:, g * 256 : g * 256 + 256] for g in range(8)], axis=0
        ).astype(BF16)
        back_cols = jnp.dot(heat, from_columns, preferred_element_type=F32)
        for h in range(2):
            quads = [
                swap_chunks(
                    [
                        back_cols[
                            (h * 4 + g) * 32 : (h * 4 + g) * 32 + 32, yh * 128 : yh * 128 + 128
                        ]
                        for g in range(4)
                    ]
                )
                for yh in range(2)
            ]
            flat = [p.reshape(4, 8, 128) for p in quads[0] + quads[1]]
            for y in range(0, 8, 2):
                hs_ref[pl.ds(z * 4, 4), h * 64 + y * 8 : h * 64 + y * 8 + 16, :] = (
                    jnp.concatenate([flat[y], flat[y + 1]], axis=1).astype(BF16)
                )
    for q in range(nz):
        z = (mz - q + nz) % nz
        s0 = z * 32
        for d in range(4):
            if q == 0 and d == 0:
                own.wait()
            else:
                arrival(z * 4 + (mq - d + 4) % 4).wait_recv()
        blk = recv_ref[pl.ds(z * 4, 4), :, :].astype(F32)
        rows = []
        for h in range(2):
            quads = []
            for yh in range(2):
                quads.append(
                    swap_chunks(
                        [
                            blk[:, h * 64 + y * 8 : h * 64 + y * 8 + 8, :].reshape(32, 128)
                            for y in range(yh * 4, yh * 4 + 4)
                        ]
                    )
                )
            for g in range(4):
                rows.append(jnp.concatenate([quads[0][g], quads[1][g]], axis=1))
        cols = jnp.dot(
            jnp.concatenate(rows, axis=0).astype(BF16),
            to_columns,
            preferred_element_type=F32,
        )
        for g in range(8):
            tmp_ref[:, g * 256 : g * 256 + 256] = cols[g * 32 : g * 32 + 32]

        got = axr_ref[pl.ds(z * 4, 4), :, :].astype(F32)
        la = got[:, 0:8, :].reshape(32, 128)
        cnt = got[:, 8:16, :].reshape(32, 128)
        amb = jnp.where(upper, la, pltpu.roll(la, 64, 1))
        wet = cnt - level
        kap_prev = jnp.zeros((32, 128), F32)
        t_next = tmp_ref[:, 0:128]
        tr_next = pltpu.roll(t_next, 64, 1)
        for i in range(16):
            t_i, tr_i = t_next, tr_next
            if i < 15:
                t_next = tmp_ref[:, 128 * i + 128 : 128 * i + 256]
                tr_next = pltpu.roll(t_next, 64, 1)
                t_below = jnp.where(upper, tr_next, tr_i)
            else:
                t_below = jnp.where(upper, t_i, tr_i)
            top = top_ref[i, pl.ds(s0, 32), :]
            growth = jnp.exp(GROWTH_TEMP * t_i) * top / (top + 1.0)
            gv_ref[i, pl.ds(s0, 32)] = jnp.where(wet > 2.0 * i, STEP_DT * growth, 0.0)
            kap = amb * (1.0 + 0.5 * jnp.tanh(t_i - t_below))
            kap = jnp.where(wet > 2.0 * i + 1.0, STEP_DT * kap, 0.0)
            kap_r = pltpu.roll(kap, 64, 1)
            kap_ref[i, pl.ds(s0, 32)] = kap
            kup_ref[i, pl.ds(s0, 32)] = jnp.where(upper, kap_r, kap_prev)
            kap_prev = kap_r

        for g in range(8):
            at = slice(256 * g, 256 * g + 256)
            c_b = c_ref[pl.ds(s0, 32), :, at].reshape(256, 256).astype(BF16)
            mix_ref[pl.ds(pl.multiple_of(s0 * 8, 256), 256), at] = jnp.dot(mat_hi, c_b, preferred_element_type=F32) + jnp.dot(
                mat_lo, c_b, preferred_element_type=F32
            )

        def grow(step, acc):
            acc = list(acc)
            for u in range(UNROLL):
                s = s0 + step * UNROLL + u
                for i in range(16):
                    acc[i % 4] = acc[i % 4] + row_of(gv_ref, i, s) * mix_of(i, s)
            return tuple(acc)

        sums = lax.fori_loop(0, 32 // UNROLL, grow, sums)
    gx_sums(sums)

    own_back.start()
    for d in range(1, gy_n):
        back((my + d) % gy_n).start()

    def tracers(step, carry):
        for u in range(UNROLL):
            s = step * UNROLL + u
            c_next = c_ref[s, :, 0:128]
            cr_next = pltpu.roll(c_next, 64, 1)
            cr_i = cr_next
            for i in range(16):
                at = slice(128 * i, 128 * i + 128)
                cr_prev = cr_i
                c_i, cr_i = c_next, cr_next
                if i < 15:
                    c_next = c_ref[s, :, 128 * i + 128 : 128 * i + 256]
                    cr_next = pltpu.roll(c_next, 64, 1)
                below = jnp.where(upper8, cr_next, cr_i)
                above = jnp.where(upper8, cr_i, cr_prev)
                grown = row_of(gv_ref, i, s) * mix_of(i, s)
                pre_ref[s, :, at] = (c_i + row_of(kap_ref, i, s) * (below - c_i)) + (
                    row_of(kup_ref, i, s) * (above - c_i) + grown
                )
        return carry

    steps = slots // UNROLL
    lax.fori_loop(0, steps // 2, tracers, 0)
    for d in range(1, gx_n):
        gx_arrival((mx + d) % gx_n).wait_recv()
    ar_ref[1] = jnp.sum(ara_ref[...], axis=0)
    for d in range(1, gy_n):
        gy_send((my + d) % gy_n).start()
    arb_ref[my] = ar_ref[1]
    lax.fori_loop(steps // 2, steps, tracers, 0)

    for q in range(nz):
        z = (mz + q) % nz
        for d in range(4):
            if q == 0 and d == 0:
                own_back.wait()
            else:
                back_arrival(z * 4 + (mq + d) % 4).wait_recv()
        got = hr_ref[pl.ds(z * 4, 4), :, :]
        sel = sel_ref[pl.ds(pl.multiple_of(z * 256, 256), 256), :]
        for h in range(2):
            lhs = got[:, h * 64 : h * 64 + 64, :].reshape(256, 128)
            warm = lax.dot_general(lhs, sel, TN, preferred_element_type=F32)
            rows_h = slice(128 * h, 128 * h + 128)
            if q == 0:
                warm_ref[rows_h, :] = warm
            else:
                warm_ref[rows_h, :] = warm_ref[rows_h, :] + warm

    def finish(k, carry):
        part = warm_ref[pl.ds(pl.multiple_of(k * 8, 8), 8), :]
        for bx in range(4):
            therm_ref[k, 8 * bx : 8 * bx + 8, :] = (
                step_ref[k, 8 * bx : 8 * bx + 8, :]
                + WARMING_SCALE * part[:, 128 * bx : 128 * bx + 128]
            )
        return carry

    lax.fori_loop(0, LEVELS, finish, 0)

    for copy in halos:
        copy.wait_send()
    for d in range(1, gy_n):
        forward((my + d) % gy_n).wait_send()
        back((my + d) % gy_n).wait_send()
        aux_send((my + d) % gy_n).wait_send()
    for d in range(1, gx_n):
        gx_send((mx + d) % gx_n).wait_send()

    for d in range(1, gy_n):
        gy_arrival((my + d) % gy_n).wait_recv()
    total = jnp.sum(arb_ref[...], axis=0)
    grown = jnp.sum(total[0:8], axis=1, keepdims=True)
    shift_ref[...] = -(jnp.broadcast_to(grown, (8, 128)) / jnp.maximum(total[8:16], 1.0))

    for d in range(1, gy_n):
        gy_send((my + d) % gy_n).wait_send()


def finish_kernel(pre_ref, cnt_ref, shift_ref, therm_ref, out_ref, thout_ref, buf_ref, sem):
    level = jnp.where(iota((8, 128), 1) >= 64, 1.0, 0.0)
    n = pre_ref.shape[0] // OUT_CHUNK
    thermal = pltpu.make_async_copy(therm_ref, thout_ref, sem.at[OUT_BUFS])
    thermal.start()
    shift = shift_ref[...]

    def out_copy(c):
        return pltpu.make_async_copy(
            buf_ref.at[c % OUT_BUFS],
            out_ref.at[pl.ds(c * OUT_CHUNK, OUT_CHUNK)],
            sem.at[c % OUT_BUFS],
        )

    for c in range(n):
        if c >= OUT_BUFS:
            out_copy(c - OUT_BUFS).wait()

        def some(step, carry):
            for u in range(OUT_STEP):
                s = step * OUT_STEP + u
                wet = cnt_ref[pl.ds(c * OUT_CHUNK + s, 8, stride=0), :] - level
                for i in range(16):
                    at = slice(128 * i, 128 * i + 128)
                    buf_ref[c % OUT_BUFS, s, :, at] = pre_ref[
                        c * OUT_CHUNK + s, :, at
                    ] + jnp.where(wet > 2.0 * i, shift, 0.0)
            return carry

        lax.fori_loop(0, OUT_CHUNK // OUT_STEP, some, 0)
        out_copy(c).start()
    for c in range(max(n - OUT_BUFS, 0), n):
        out_copy(c).wait()
    thermal.wait()


def solution(mesh):
    gx_n = mesh.shape["gx"]
    gy_n = mesh.shape["gy"]
    slots = 8 * gy_n

    def on_device(thermal, amb, light, flags, tally, hold, solutes, rates):
        dma = pltpu.SemaphoreType.DMA
        vmem = pl.BlockSpec(memory_space=pltpu.VMEM)
        hbm = pl.BlockSpec(memory_space=pltpu.HBM)
        tracers = solutes.reshape(slots, 8, 2048)
        pre, cnt, shift, therm = pl.pallas_call(
            functools.partial(exchange_kernel, gx_n, gy_n),
            out_shape=[
                pltpu.VMEM((slots, 8, 2048), F32),
                pltpu.VMEM((slots + 8, 128), F32),
                pltpu.VMEM((8, 128), F32),
                pltpu.VMEM((32, 32, 128), F32),
            ],
            in_specs=[hbm] * 8,
            out_specs=[vmem] * 4,
            scratch_shapes=[
                pltpu.VMEM((32, 32, 128), F32),
                pltpu.VMEM((32, 128), BF16),
                pltpu.VMEM((32, 128), BF16),
                pltpu.VMEM((1, BLOCKS), jnp.int32),
                pltpu.VMEM((1, BLOCKS), jnp.int32),
                pltpu.VMEM((1, BLOCKS), jnp.int32),
                pltpu.VMEM((8, 8), F32),
                pltpu.VMEM((slots, 8, 2048), F32),
                pltpu.VMEM((64 * gy_n, 512), BF16),
                pltpu.VMEM((256, 512), BF16),
                pltpu.VMEM((32, 32, 128), F32),
                pltpu.VMEM((gy_n, 128, 128), BF16),
                pltpu.VMEM((gy_n, 128, 128), BF16),
                pltpu.VMEM((gy_n, 16, 128), BF16),
                pltpu.VMEM((gy_n, 16, 128), BF16),
                pltpu.VMEM((16, slots, 128), F32),
                pltpu.VMEM((gy_n, 128, 128), BF16),
                pltpu.VMEM((gy_n, 128, 128), BF16),
                pltpu.VMEM((32, 2048), F32),
                pltpu.VMEM((32, 2048), F32),
                pltpu.VMEM((16, slots + 8, 128), F32),
                pltpu.VMEM((16, slots + 8, 128), F32),
                pltpu.VMEM((16, slots + 8, 128), F32),
                pltpu.VMEM((8 * slots, 2048), F32),
                pltpu.VMEM((256, 512), F32),
                pltpu.VMEM((2, 40, 128), F32),
                pltpu.VMEM((2, 40, 128), F32),
                pltpu.VMEM((2, 16, 128), F32),
                pltpu.VMEM((2, 16, 128), F32),
                pltpu.VMEM((2, 16, 128), F32),
                pltpu.VMEM((gx_n, 16, 128), F32),
                pltpu.VMEM((gy_n, 16, 128), F32),
                dma((7,)),
                dma((gy_n // 4,)),
                dma((4,)),
                dma((4,)),
                dma((gy_n,)),
                dma((gy_n,)),
                dma((gy_n,)),
                dma((gy_n,)),
                dma((3,)),
                dma((gy_n,)),
                dma((gy_n,)),
                dma((gx_n,)),
                dma((gx_n,)),
                dma((gy_n,)),
                dma((gy_n,)),
            ],
            compiler_params=pltpu.CompilerParams(
                collective_id=0, has_side_effects=True, vmem_limit_bytes=40 * 1024 * 1024
            ),
            name="exchange",
        )(
            *(
                pltpu.with_memory_space_constraint(a, pltpu.HBM)
                for a in (
                    thermal,
                    amb,
                    light,
                    flags.reshape(1, BLOCKS),
                    tally.reshape(1, BLOCKS),
                    hold.reshape(1, BLOCKS),
                    rates,
                    tracers,
                )
            )
        )
        out, therm_out = pl.pallas_call(
            finish_kernel,
            out_shape=[
                jax.ShapeDtypeStruct((slots, 8, 2048), F32),
                jax.ShapeDtypeStruct((32, 32, 128), F32),
            ],
            in_specs=[vmem] * 4,
            out_specs=[hbm] * 2,
            scratch_shapes=[
                pltpu.VMEM((OUT_BUFS, OUT_CHUNK, 8, 2048), F32),
                dma((OUT_BUFS + 1,)),
            ],
            compiler_params=pltpu.CompilerParams(vmem_limit_bytes=16 * 1024 * 1024),
            name="finish",
        )(pre, cnt, shift, therm)
        return therm_out, out.reshape(solutes.shape)

    return jax.shard_map(
        on_device,
        mesh=mesh,
        in_specs=(
            P(None, "gx", "gy"),
            P("gx", "gy"),
            P("gx", "gy"),
            P("gx", "gy", None),
            P("gx", "gy", None),
            P("gx", "gy", None, None),
            P("gx", "gy", None, None, None),
            P(),
        ),
        out_specs=(P(None, "gx", "gy"), P("gx", "gy", None, None, None)),
        check_vma=False,
    )
```

```python
import functools

import jax
import jax.numpy as jnp
from jax import lax
from jax.experimental import pallas as pl
from jax.experimental.pallas import tpu as pltpu
from jax.sharding import PartitionSpec as P

MESH = pl.DeviceIdType.MESH
F32 = jnp.float32
BF16 = jnp.bfloat16

NU_COEF = 0.2
STEP_DT = 0.05
ATTEN_WATER = 0.06
ATTEN_CHL = 0.05
WARMING_SCALE = 0.5
GROWTH_TEMP = 0.063

LEVELS = 32
BLOCKS = 64
UNROLL = 4
LEVEL_STEP = 8
OUT_STEP = 8
OUT_CHUNK = 16
OUT_BUFS = 8
NT = (((1,), (1,)), ((), ()))
TN = (((0,), (0,)), ((), ()))


def iota(shape, dim):
    return lax.broadcasted_iota(jnp.int32, shape, dim)


def one_hot(mask):
    return jnp.where(mask, 1.0, 0.0).astype(BF16)


def swap_chunks(parts):
    lane = iota(parts[0].shape, 1)
    low = lane < 64
    even = (lane & 32) == 0
    a, b, c, d = parts
    a, c = jnp.where(low, a, pltpu.roll(c, 64, 1)), jnp.where(low, pltpu.roll(a, 64, 1), c)
    b, d = jnp.where(low, b, pltpu.roll(d, 64, 1)), jnp.where(low, pltpu.roll(b, 64, 1), d)
    a, b = jnp.where(even, a, pltpu.roll(b, 32, 1)), jnp.where(even, pltpu.roll(a, 96, 1), b)
    c, d = jnp.where(even, c, pltpu.roll(d, 32, 1)), jnp.where(even, pltpu.roll(c, 96, 1), d)
    return [a, b, c, d]


def exchange_kernel(
    gx_n,
    gy_n,
    t_hbm,
    amb_hbm,
    light_hbm,
    flag_hbm,
    tally_hbm,
    hold_hbm,
    rate_hbm,
    c_hbm,
    pre_ref,
    cnt_ref,
    shift_ref,
    therm_ref,
    t_ref,
    amb_ref,
    light_ref,
    flag_ref,
    tally_ref,
    hold_ref,
    rate_ref,
    c_ref,
    sel_ref,
    ut_ref,
    step_ref,
    pay_ref,
    recv_ref,
    ax_ref,
    axr_ref,
    top_ref,
    hs_ref,
    hr_ref,
    tmp_ref,
    heat_ref,
    kap_ref,
    kup_ref,
    gv_ref,
    mix_ref,
    warm_ref,
    hxs_ref,
    hxr_ref,
    hys_ref,
    hyr_ref,
    ar_ref,
    ara_ref,
    arb_ref,
    in_sem,
    c_sem,
    halo_s,
    halo_r,
    xs_sem,
    xr_sem,
    fs_sem,
    fr_sem,
    own_sem,
    bs_sem,
    br_sem,
    as_sem,
    ar_sem,
    gs_sem,
    gr_sem,
):
    nz = gy_n // 4
    mx = lax.axis_index("gx")
    my = lax.axis_index("gy")
    mz = my // 4
    mq = my % 4

    def c_copy(z):
        return pltpu.make_async_copy(
            c_hbm.at[pl.ds(z * 32, 32)], c_ref.at[pl.ds(z * 32, 32)], c_sem.at[z]
        )

    loads = [
        pltpu.make_async_copy(src, dst, in_sem.at[n])
        for n, (src, dst) in enumerate(
            (
                (t_hbm, t_ref),
                (flag_hbm, flag_ref),
                (tally_hbm, tally_ref),
                (hold_hbm, hold_ref),
                (amb_hbm, amb_ref),
                (light_hbm, light_ref),
                (rate_hbm, rate_ref),
            )
        )
    ]
    for copy in loads:
        copy.start()

    bar = pltpu.get_barrier_semaphore()
    for d in range(1, gx_n):
        pl.semaphore_signal(
            bar, 1, device_id={"gx": (mx + d) % gx_n}, device_id_type=MESH
        )
    for d in range(1, gy_n):
        pl.semaphore_signal(
            bar, 1, device_id={"gy": (my + d) % gy_n}, device_id_type=MESH
        )

    for copy in loads:
        copy.wait()
    for q in range(nz):
        c_copy((mz - q + nz) % nz).start()

    dep = (flag_ref[...] * tally_ref[...]).astype(F32)
    hold = hold_ref[...].astype(F32)
    bi = iota((BLOCKS, BLOCKS), 0)
    bj = iota((BLOCKS, BLOCKS), 1)
    hold_b = jnp.broadcast_to(hold, (BLOCKS, BLOCKS))
    hold_c = jnp.sum(jnp.where(bi == bj, hold_b, 0.0), axis=1, keepdims=True)
    same = jnp.where((hold_c == hold_b) & (bi < bj), 1.0, 0.0)
    rank = jnp.sum(same, axis=0, keepdims=True)
    slot = hold * 8.0 + rank
    r8 = iota((8, BLOCKS), 0)
    pair = jnp.where(
        r8 == 0,
        jnp.broadcast_to(slot, (8, BLOCKS)),
        jnp.where(r8 == 1, jnp.broadcast_to(dep, (8, BLOCKS)), 0.0),
    ).astype(BF16)
    spread = one_hot(iota((BLOCKS, 512), 0) == (iota((BLOCKS, 512), 1) >> 3))
    lanes = jnp.dot(pair, spread, preferred_element_type=F32)
    slot_l = lanes[0:1]
    dep_l = lanes[1:2]
    lane8 = iota((8, 128), 1)
    dep_b = [
        jnp.broadcast_to(dep_l[:, 128 * bx : 128 * bx + 128], (8, 128)) for bx in range(4)
    ]
    cells = jnp.sum(dep, axis=1, keepdims=True) * 64.0

    hxs_ref[0, 0:32, :] = t_ref[:, 0, :]
    hxs_ref[1, 0:32, :] = t_ref[:, 31, :]
    hxs_ref[0, 32:40, :] = dep_b[0]
    hxs_ref[1, 32:40, :] = dep_b[3]

    zero8 = jnp.zeros((8, 128), F32)
    low4, high4 = [zero8] * 4, [zero8] * 4
    for k in range(LEVELS):
        for bx in range(4):
            part = t_ref[k, 8 * bx : 8 * bx + 8, :]
            place = 32 * bx + k
            low4[bx] = jnp.where(lane8 == place, pltpu.roll(part, place, 1), low4[bx])
            high4[bx] = jnp.where(
                lane8 == place, pltpu.roll(part, (place + 1) % 128, 1), high4[bx]
            )
    quarter = lane8 >> 5
    low = jnp.where(
        quarter < 2,
        jnp.where(quarter == 0, low4[0], low4[1]),
        jnp.where(quarter == 2, low4[2], low4[3]),
    )
    high = jnp.where(
        quarter < 2,
        jnp.where(quarter == 0, high4[0], high4[1]),
        jnp.where(quarter == 2, high4[2], high4[3]),
    )
    dlow, dhigh = zero8, zero8
    for bx in range(4):
        dlow = jnp.where(lane8 == 32 * bx, pltpu.roll(dep_b[bx], 32 * bx, 1), dlow)
        dhigh = jnp.where(lane8 == 32 * bx, pltpu.roll(dep_b[bx], 32 * bx + 1, 1), dhigh)
    hys_ref[0, 0:8, :] = low
    hys_ref[1, 0:8, :] = high
    hys_ref[0, 8:16, :] = dlow
    hys_ref[1, 8:16, :] = dhigh

    pl.semaphore_wait(bar, gx_n - 1 + gy_n - 1)

    def halo(side):
        step = gx_n - 1 if side == 0 else 1
        stepy = gy_n - 1 if side == 0 else 1
        return (
            pltpu.make_async_remote_copy(
                hxs_ref.at[side],
                hxr_ref.at[1 - side],
                halo_s.at[side],
                halo_r.at[side],
                device_id={"gx": (mx + step) % gx_n},
                device_id_type=MESH,
            ),
            pltpu.make_async_remote_copy(
                hys_ref.at[side],
                hyr_ref.at[1 - side],
                halo_s.at[2 + side],
                halo_r.at[2 + side],
                device_id={"gy": (my + stepy) % gy_n},
                device_id_type=MESH,
            ),
        )

    halos = halo(0) + halo(1)
    for copy in halos:
        copy.start()

    def by_lanes(field):
        return jnp.concatenate([field[8 * bx : 8 * bx + 8] for bx in range(4)], axis=1)

    aux = jnp.concatenate(
        [
            by_lanes(light_ref[...].astype(F32)),
            by_lanes(amb_ref[...].astype(F32)),
            jnp.broadcast_to(dep_l, (8, 512)),
            jnp.zeros((8, 512), F32),
        ],
        axis=0,
    ).astype(BF16)
    er = iota((256, 32), 0)
    ef = iota((256, 32), 1)
    place = one_hot(ef == jnp.where(er < 128, er >> 3, 16))
    wide = jnp.dot(place, aux, preferred_element_type=F32)
    wide = jnp.where(
        (iota((256, 512), 0) & 7) == (iota((256, 512), 1) & 7), wide, 0.0
    ).astype(BF16)
    slots = 8 * gy_n
    sel_b = one_hot(
        iota((slots, 512), 0).astype(F32) == jnp.broadcast_to(slot_l, (slots, 512))
    )
    packed_aux = lax.dot_general(sel_b, wide, NT, preferred_element_type=F32)
    packed_aux = packed_aux.reshape(gy_n, 8, 256)
    ax_ref[...] = jnp.concatenate(
        [packed_aux[:, :, :128], packed_aux[:, :, 128:]], axis=1
    ).astype(BF16)

    def aux_send(other):
        return pltpu.make_async_remote_copy(
            ax_ref.at[other],
            axr_ref.at[my],
            xs_sem.at[other],
            xr_sem.at[my],
            device_id={"gy": other},
            device_id_type=MESH,
        )

    def aux_arrival(other):
        return pltpu.make_async_remote_copy(
            ax_ref.at[other],
            axr_ref.at[other],
            xs_sem.at[other],
            xr_sem.at[other],
            device_id={"gy": other},
            device_id_type=MESH,
        )

    own_aux = pltpu.make_async_copy(ax_ref.at[my], axr_ref.at[my], own_sem.at[2])
    own_aux.start()
    for d in range(1, gy_n):
        aux_send((my + d) % gy_n).start()

    lane_n = iota((1, 512), 1)
    key_l = slot_l * 8.0 + (lane_n & 7).astype(F32)

    def build_sel(z, carry):
        m = iota((256, 1), 0) + z * 256
        key = ((m >> 6) << 6) | ((m & 7) << 3) | ((m >> 3) & 7)
        sel_ref[pl.ds(pl.multiple_of(z * 256, 256), 256), :] = one_hot(
            jnp.broadcast_to(key.astype(F32), (256, 512))
            == jnp.broadcast_to(key_l, (256, 512))
        )
        return carry

    lax.fori_loop(0, nz, build_sel, 0)

    for copy in halos:
        copy.wait_recv()

    row = iota((32, 128), 0)
    lane = iota((32, 128), 1)
    on_low_x = jnp.where(mx > 0, 1.0, 0.0)
    on_high_x = jnp.where(mx < gx_n - 1, 1.0, 0.0)
    on_low_y = jnp.where(my > 0, 1.0, 0.0)
    on_high_y = jnp.where(my < gy_n - 1, 1.0, 0.0)

    def around(field, below_row, above_row, low_h, high_h):
        up = jnp.where(row == 0, below_row, pltpu.roll(field, 1, 0))
        down = jnp.where(row == 31, above_row, pltpu.roll(field, 31, 0))
        low_v = jnp.concatenate(
            [low_h] + [pltpu.roll(low_h, 128 - 32 * bx, 1) for bx in (1, 2, 3)], axis=0
        )
        high_v = jnp.concatenate(
            [pltpu.roll(high_h, 127 - 32 * bx, 1) for bx in range(4)], axis=0
        )
        west = jnp.where(lane == 0, low_v, pltpu.roll(field, 1, 1))
        east = jnp.where(lane == 127, high_v, pltpu.roll(field, 127, 1))
        return up, down, west, east

    dep2 = jnp.concatenate(dep_b, axis=0)
    dep_n = around(
        dep2,
        hxr_ref[0, 32:33, :] * on_low_x,
        hxr_ref[1, 32:33, :] * on_high_x,
        hyr_ref[0, 8:16, :] * on_low_y,
        hyr_ref[1, 8:16, :] * on_high_y,
    )

    def stencil(kk, carry):
        low_h, high_h = carry
        done = []
        for part in range(LEVEL_STEP):
            k = kk * LEVEL_STEP + part
            field = t_ref[k]
            near = around(
                field,
                hxr_ref[0, pl.ds(k, 1), :],
                hxr_ref[1, pl.ds(k, 1), :],
                low_h,
                high_h,
            )
            low_h = pltpu.roll(low_h, 127, 1)
            high_h = pltpu.roll(high_h, 127, 1)
            kf = k.astype(F32)
            total = jnp.where(dep_n[0] > kf, near[0] - field, 0.0)
            for d, n in zip(dep_n[1:], near[1:]):
                total = total + jnp.where(d > kf, n - field, 0.0)
            stepped = field + NU_COEF * jnp.where(dep2 > kf, total, 0.0)
            step_ref[k] = stepped
            done.append(stepped)
        size = 8 * LEVEL_STEP
        rows = pl.ds(pl.multiple_of(kk * size, size), size)
        for bx in range(4):
            ut_ref[rows, 128 * bx : 128 * bx + 128] = jnp.concatenate(
                [d[8 * bx : 8 * bx + 8] for d in done], axis=0
            ).astype(BF16)
        return low_h, high_h

    lax.fori_loop(
        0, LEVELS // LEVEL_STEP, stencil, (hyr_ref[0, 0:8, :], hyr_ref[1, 0:8, :]))

    def forward(other):
        return pltpu.make_async_remote_copy(
            pay_ref.at[other],
            recv_ref.at[my],
            fs_sem.at[other],
            fr_sem.at[my],
            device_id={"gy": other},
            device_id_type=MESH,
        )

    def arrival(other):
        return pltpu.make_async_remote_copy(
            pay_ref.at[other],
            recv_ref.at[other],
            fs_sem.at[other],
            fr_sem.at[other],
            device_id={"gy": other},
            device_id_type=MESH,
        )

    own = pltpu.make_async_copy(pay_ref.at[my], recv_ref.at[my], own_sem.at[0])
    for q in range(nz):
        z = (mz + q) % nz
        part = lax.dot_general(
            sel_ref[pl.ds(pl.multiple_of(z * 256, 256), 256), :],
            ut_ref[...],
            NT,
            preferred_element_type=F32,
        ).astype(BF16)
        part = part.reshape(4, 64, 256)
        pay_ref[pl.ds(z * 4, 4), 0:64, :] = part[:, :, :128]
        pay_ref[pl.ds(z * 4, 4), 64:128, :] = part[:, :, 128:]
        for d in range(4):
            if q == 0 and d == 0:
                own.start()
            else:
                forward(z * 4 + (mq + d) % 4).start()

    pi = iota((256, 256), 0)
    po = iota((256, 256), 1)
    to_columns = one_hot(po == (((pi & 31) << 3) | (pi >> 5)))
    from_columns = one_hot(pi == (((po & 31) << 3) | (po >> 5)))
    rates = jnp.concatenate([rate_ref[...]] * 32, axis=0)
    spread_r = (iota((8, 256), 1) & 7) == iota((8, 256), 0)
    rates_hi = rates.astype(BF16)
    rates_lo = (rates - rates_hi.astype(F32)).astype(BF16)
    spread_r = one_hot(spread_r)
    diagonal = (pi >> 3) == (po >> 3)
    mat_hi = jnp.where(
        diagonal, jnp.dot(rates_hi, spread_r, preferred_element_type=F32), 0.0
    ).astype(BF16)
    mat_lo = jnp.where(
        diagonal, jnp.dot(rates_lo, spread_r, preferred_element_type=F32), 0.0
    ).astype(BF16)
    upper = lane >= 64
    upper8 = lane8 >= 64
    level = jnp.where(upper, 1.0, 0.0)
    sums = (zero8,) * 4

    def back(other):
        return pltpu.make_async_remote_copy(
            hs_ref.at[other],
            hr_ref.at[my],
            bs_sem.at[other],
            br_sem.at[my],
            device_id={"gy": other},
            device_id_type=MESH,
        )

    def back_arrival(other):
        return pltpu.make_async_remote_copy(
            hs_ref.at[other],
            hr_ref.at[other],
            bs_sem.at[other],
            br_sem.at[other],
            device_id={"gy": other},
            device_id_type=MESH,
        )

    own_back = pltpu.make_async_copy(hs_ref.at[my], hr_ref.at[my], own_sem.at[1])

    def gx_send(other):
        return pltpu.make_async_remote_copy(
            ar_ref.at[0],
            ara_ref.at[mx],
            as_sem.at[other],
            ar_sem.at[mx],
            device_id={"gx": other},
            device_id_type=MESH,
        )

    def gx_arrival(other):
        return pltpu.make_async_remote_copy(
            ar_ref.at[0],
            ara_ref.at[other],
            as_sem.at[other],
            ar_sem.at[other],
            device_id={"gx": other},
            device_id_type=MESH,
        )

    def gy_send(other):
        return pltpu.make_async_remote_copy(
            ar_ref.at[1],
            arb_ref.at[my],
            gs_sem.at[other],
            gr_sem.at[my],
            device_id={"gy": other},
            device_id_type=MESH,
        )

    def gy_arrival(other):
        return pltpu.make_async_remote_copy(
            ar_ref.at[1],
            arb_ref.at[other],
            gs_sem.at[other],
            gr_sem.at[other],
            device_id={"gy": other},
            device_id_type=MESH,
        )

    def gx_sums(sums):
        ar_ref[0, 0:8, :] = (sums[0] + sums[1]) + (sums[2] + sums[3])
        ar_ref[0, 8:16, :] = jnp.broadcast_to(cells, (8, 128))
        for d in range(1, gx_n):
            gx_send((mx + d) % gx_n).start()
        ara_ref[mx] = ar_ref[0]

    def row_of(ref, i, s):
        return ref[i, pl.ds(s, 8, stride=0), :]

    def mix_of(i, s):
        return mix_ref[pl.ds(pl.multiple_of(s * 8, 8), 8), 128 * i : 128 * i + 128]

    for q in range(nz):
        z = (mz - q + nz) % nz
        s0 = z * 32
        for d in range(4):
            if q == 0 and d == 0:
                own_aux.wait()
            else:
                aux_arrival(z * 4 + (mq - d + 4) % 4).wait_recv()
        c_copy(z).wait()
        got = axr_ref[pl.ds(z * 4, 4), :, :].astype(F32)
        la = got[:, 0:8, :].reshape(32, 128)
        cnt = got[:, 8:16, :].reshape(32, 128)
        cnt_ref[pl.ds(s0, 32), :] = cnt
        light = jnp.where(upper, pltpu.roll(la, 64, 1), la)
        run = jnp.zeros((32, 128), F32)
        prev = light
        wet = cnt - level
        for i in range(16):
            at = slice(128 * i, 128 * i + 128)
            atten = ATTEN_WATER + ATTEN_CHL * c_ref[pl.ds(s0, 32), 0, at]
            both = atten + pltpu.roll(atten, 64, 1)
            cum = run + jnp.where(upper, both, atten)
            run = run + both
            bottom = light * jnp.exp(-cum)
            bottom_r = pltpu.roll(bottom, 64, 1)
            top = jnp.where(upper, bottom_r, prev)
            prev = bottom_r
            top_ref[i, pl.ds(s0, 32), :] = top
            heat_ref[:, at] = jnp.where(wet > 2.0 * i, top - bottom, 0.0)
        for g in range(8):
            at = slice(256 * g, 256 * g + 256)
            c_b = c_ref[pl.ds(s0, 32), :, at].reshape(256, 256).astype(BF16)
            mix_ref[pl.ds(pl.multiple_of(s0 * 8, 256), 256), at] = jnp.dot(mat_hi, c_b, preferred_element_type=F32) + jnp.dot(
                mat_lo, c_b, preferred_element_type=F32
            )

        heat = jnp.concatenate(
            [heat_ref[:, g * 256 : g * 256 + 256] for g in range(8)], axis=0
        ).astype(BF16)
        back_cols = jnp.dot(heat, from_columns, preferred_element_type=F32)
        for h in range(2):
            quads = [
                swap_chunks(
                    [
                        back_cols[
                            (h * 4 + g) * 32 : (h * 4 + g) * 32 + 32, yh * 128 : yh * 128 + 128
                        ]
                        for g in range(4)
                    ]
                )
                for yh in range(2)
            ]
            flat = [p.reshape(4, 8, 128) for p in quads[0] + quads[1]]
            for y in range(0, 8, 2):
                hs_ref[pl.ds(z * 4, 4), h * 64 + y * 8 : h * 64 + y * 8 + 16, :] = (
                    jnp.concatenate([flat[y], flat[y + 1]], axis=1).astype(BF16)
                )
    for q in range(nz):
        z = (mz - q + nz) % nz
        s0 = z * 32
        for d in range(4):
            if q == 0 and d == 0:
                own.wait()
            else:
                arrival(z * 4 + (mq - d + 4) % 4).wait_recv()
        blk = recv_ref[pl.ds(z * 4, 4), :, :].astype(F32)
        rows = []
        for h in range(2):
            quads = []
            for yh in range(2):
                quads.append(
                    swap_chunks(
                        [
                            blk[:, h * 64 + y * 8 : h * 64 + y * 8 + 8, :].reshape(32, 128)
                            for y in range(yh * 4, yh * 4 + 4)
                        ]
                    )
                )
            for g in range(4):
                rows.append(jnp.concatenate([quads[0][g], quads[1][g]], axis=1))
        cols = jnp.dot(
            jnp.concatenate(rows, axis=0).astype(BF16),
            to_columns,
            preferred_element_type=F32,
        )
        for g in range(8):
            tmp_ref[pl.ds(s0, 32), g * 256 : g * 256 + 256] = cols[g * 32 : g * 32 + 32]

        wet = cnt_ref[pl.ds(s0, 32), :] - level
        for i in range(16):
            at = slice(128 * i, 128 * i + 128)
            top = top_ref[i, pl.ds(s0, 32), :]
            growth = jnp.exp(GROWTH_TEMP * tmp_ref[pl.ds(s0, 32), at]) * top / (top + 1.0)
            gv_ref[i, pl.ds(s0, 32)] = jnp.where(wet > 2.0 * i, STEP_DT * growth, 0.0)

        def grow(step, acc):
            acc = list(acc)
            for u in range(UNROLL):
                s = s0 + step * UNROLL + u
                for i in range(16):
                    acc[i % 4] = acc[i % 4] + row_of(gv_ref, i, s) * mix_of(i, s)
            return tuple(acc)

        sums = lax.fori_loop(0, 32 // UNROLL, grow, sums)
    gx_sums(sums)

    own_back.start()
    for d in range(1, gy_n):
        back((my + d) % gy_n).start()

    def diffusion(z):
        s0 = z * 32
        la = axr_ref[pl.ds(z * 4, 4), 0:8, :].astype(F32).reshape(32, 128)
        amb = jnp.where(upper, la, pltpu.roll(la, 64, 1))
        wet = cnt_ref[pl.ds(s0, 32), :] - level
        kap_prev = jnp.zeros((32, 128), F32)
        t_next = tmp_ref[pl.ds(s0, 32), 0:128]
        tr_next = pltpu.roll(t_next, 64, 1)
        for i in range(16):
            t_i, tr_i = t_next, tr_next
            if i < 15:
                t_next = tmp_ref[pl.ds(s0, 32), 128 * i + 128 : 128 * i + 256]
                tr_next = pltpu.roll(t_next, 64, 1)
                t_below = jnp.where(upper, tr_next, tr_i)
            else:
                t_below = jnp.where(upper, t_i, tr_i)
            kap = amb * (1.0 + 0.5 * jnp.tanh(t_i - t_below))
            kap = jnp.where(wet > 2.0 * i + 1.0, STEP_DT * kap, 0.0)
            kap_r = pltpu.roll(kap, 64, 1)
            kap_ref[i, pl.ds(s0, 32)] = kap
            kup_ref[i, pl.ds(s0, 32)] = jnp.where(upper, kap_r, kap_prev)
            kap_prev = kap_r

    for z in range(nz):
        diffusion(z)

    def tracers(step, carry):
        for u in range(UNROLL):
            s = step * UNROLL + u
            c_next = c_ref[s, :, 0:128]
            cr_next = pltpu.roll(c_next, 64, 1)
            cr_i = cr_next
            for i in range(16):
                at = slice(128 * i, 128 * i + 128)
                cr_prev = cr_i
                c_i, cr_i = c_next, cr_next
                if i < 15:
                    c_next = c_ref[s, :, 128 * i + 128 : 128 * i + 256]
                    cr_next = pltpu.roll(c_next, 64, 1)
                below = jnp.where(upper8, cr_next, cr_i)
                above = jnp.where(upper8, cr_i, cr_prev)
                grown = row_of(gv_ref, i, s) * mix_of(i, s)
                pre_ref[s, :, at] = (c_i + row_of(kap_ref, i, s) * (below - c_i)) + (
                    row_of(kup_ref, i, s) * (above - c_i) + grown
                )
        return carry

    steps = slots // UNROLL
    lax.fori_loop(0, steps // 4, tracers, 0)
    for d in range(1, gx_n):
        gx_arrival((mx + d) % gx_n).wait_recv()
    ar_ref[1] = jnp.sum(ara_ref[...], axis=0)
    for d in range(1, gy_n):
        gy_send((my + d) % gy_n).start()
    arb_ref[my] = ar_ref[1]
    lax.fori_loop(steps // 4, steps, tracers, 0)

    for q in range(nz):
        z = (mz + q) % nz
        for d in range(4):
            if q == 0 and d == 0:
                own_back.wait()
            else:
                back_arrival(z * 4 + (mq + d) % 4).wait_recv()
        got = hr_ref[pl.ds(z * 4, 4), :, :]
        sel = sel_ref[pl.ds(pl.multiple_of(z * 256, 256), 256), :]
        for h in range(2):
            lhs = got[:, h * 64 : h * 64 + 64, :].reshape(256, 128)
            warm = lax.dot_general(lhs, sel, TN, preferred_element_type=F32)
            rows_h = slice(128 * h, 128 * h + 128)
            if q == 0:
                warm_ref[rows_h, :] = warm
            else:
                warm_ref[rows_h, :] = warm_ref[rows_h, :] + warm

    def finish(k, carry):
        part = warm_ref[pl.ds(pl.multiple_of(k * 8, 8), 8), :]
        for bx in range(4):
            therm_ref[k, 8 * bx : 8 * bx + 8, :] = (
                step_ref[k, 8 * bx : 8 * bx + 8, :]
                + WARMING_SCALE * part[:, 128 * bx : 128 * bx + 128]
            )
        return carry

    lax.fori_loop(0, LEVELS, finish, 0)

    for copy in halos:
        copy.wait_send()
    for d in range(1, gy_n):
        forward((my + d) % gy_n).wait_send()
        back((my + d) % gy_n).wait_send()
        aux_send((my + d) % gy_n).wait_send()
    for d in range(1, gx_n):
        gx_send((mx + d) % gx_n).wait_send()

    for d in range(1, gy_n):
        gy_arrival((my + d) % gy_n).wait_recv()
    total = jnp.sum(arb_ref[...], axis=0)
    grown = jnp.sum(total[0:8], axis=1, keepdims=True)
    shift_ref[...] = -(jnp.broadcast_to(grown, (8, 128)) / jnp.maximum(total[8:16], 1.0))

    for d in range(1, gy_n):
        gy_send((my + d) % gy_n).wait_send()


def finish_kernel(pre_ref, cnt_ref, shift_ref, therm_ref, out_ref, thout_ref, buf_ref, sem):
    level = jnp.where(iota((8, 128), 1) >= 64, 1.0, 0.0)
    n = pre_ref.shape[0] // OUT_CHUNK
    thermal = pltpu.make_async_copy(therm_ref, thout_ref, sem.at[OUT_BUFS])
    thermal.start()
    shift = shift_ref[...]

    def out_copy(c):
        return pltpu.make_async_copy(
            buf_ref.at[c % OUT_BUFS],
            out_ref.at[pl.ds(c * OUT_CHUNK, OUT_CHUNK)],
            sem.at[c % OUT_BUFS],
        )

    for c in range(n):
        if c >= OUT_BUFS:
            out_copy(c - OUT_BUFS).wait()

        def some(step, carry):
            for u in range(OUT_STEP):
                s = step * OUT_STEP + u
                wet = cnt_ref[pl.ds(c * OUT_CHUNK + s, 8, stride=0), :] - level
                for i in range(16):
                    at = slice(128 * i, 128 * i + 128)
                    buf_ref[c % OUT_BUFS, s, :, at] = pre_ref[
                        c * OUT_CHUNK + s, :, at
                    ] + jnp.where(wet > 2.0 * i, shift, 0.0)
            return carry

        lax.fori_loop(0, OUT_CHUNK // OUT_STEP, some, 0)
        out_copy(c).start()
    for c in range(max(n - OUT_BUFS, 0), n):
        out_copy(c).wait()
    thermal.wait()


def solution(mesh):
    gx_n = mesh.shape["gx"]
    gy_n = mesh.shape["gy"]
    slots = 8 * gy_n

    def on_device(thermal, amb, light, flags, tally, hold, solutes, rates):
        dma = pltpu.SemaphoreType.DMA
        vmem = pl.BlockSpec(memory_space=pltpu.VMEM)
        hbm = pl.BlockSpec(memory_space=pltpu.HBM)
        tracers = solutes.reshape(slots, 8, 2048)
        pre, cnt, shift, therm = pl.pallas_call(
            functools.partial(exchange_kernel, gx_n, gy_n),
            out_shape=[
                pltpu.VMEM((slots, 8, 2048), F32),
                pltpu.VMEM((slots + 8, 128), F32),
                pltpu.VMEM((8, 128), F32),
                pltpu.VMEM((32, 32, 128), F32),
            ],
            in_specs=[hbm] * 8,
            out_specs=[vmem] * 4,
            scratch_shapes=[
                pltpu.VMEM((32, 32, 128), F32),
                pltpu.VMEM((32, 128), BF16),
                pltpu.VMEM((32, 128), BF16),
                pltpu.VMEM((1, BLOCKS), jnp.int32),
                pltpu.VMEM((1, BLOCKS), jnp.int32),
                pltpu.VMEM((1, BLOCKS), jnp.int32),
                pltpu.VMEM((8, 8), F32),
                pltpu.VMEM((slots, 8, 2048), F32),
                pltpu.VMEM((64 * gy_n, 512), BF16),
                pltpu.VMEM((256, 512), BF16),
                pltpu.VMEM((32, 32, 128), F32),
                pltpu.VMEM((gy_n, 128, 128), BF16),
                pltpu.VMEM((gy_n, 128, 128), BF16),
                pltpu.VMEM((gy_n, 16, 128), BF16),
                pltpu.VMEM((gy_n, 16, 128), BF16),
                pltpu.VMEM((16, slots, 128), F32),
                pltpu.VMEM((gy_n, 128, 128), BF16),
                pltpu.VMEM((gy_n, 128, 128), BF16),
                pltpu.VMEM((slots, 2048), F32),
                pltpu.VMEM((32, 2048), F32),
                pltpu.VMEM((16, slots + 8, 128), F32),
                pltpu.VMEM((16, slots + 8, 128), F32),
                pltpu.VMEM((16, slots + 8, 128), F32),
                pltpu.VMEM((8 * slots, 2048), F32),
                pltpu.VMEM((256, 512), F32),
                pltpu.VMEM((2, 40, 128), F32),
                pltpu.VMEM((2, 40, 128), F32),
                pltpu.VMEM((2, 16, 128), F32),
                pltpu.VMEM((2, 16, 128), F32),
                pltpu.VMEM((2, 16, 128), F32),
                pltpu.VMEM((gx_n, 16, 128), F32),
                pltpu.VMEM((gy_n, 16, 128), F32),
                dma((7,)),
                dma((gy_n // 4,)),
                dma((4,)),
                dma((4,)),
                dma((gy_n,)),
                dma((gy_n,)),
                dma((gy_n,)),
                dma((gy_n,)),
                dma((3,)),
                dma((gy_n,)),
                dma((gy_n,)),
                dma((gx_n,)),
                dma((gx_n,)),
                dma((gy_n,)),
                dma((gy_n,)),
            ],
            compiler_params=pltpu.CompilerParams(
                collective_id=0, has_side_effects=True, vmem_limit_bytes=40 * 1024 * 1024
            ),
            name="exchange",
        )(
            *(
                pltpu.with_memory_space_constraint(a, pltpu.HBM)
                for a in (
                    thermal,
                    amb,
                    light,
                    flags.reshape(1, BLOCKS),
                    tally.reshape(1, BLOCKS),
                    hold.reshape(1, BLOCKS),
                    rates,
                    tracers,
                )
            )
        )
        out, therm_out = pl.pallas_call(
            finish_kernel,
            out_shape=[
                jax.ShapeDtypeStruct((slots, 8, 2048), F32),
                jax.ShapeDtypeStruct((32, 32, 128), F32),
            ],
            in_specs=[vmem] * 4,
            out_specs=[hbm] * 2,
            scratch_shapes=[
                pltpu.VMEM((OUT_BUFS, OUT_CHUNK, 8, 2048), F32),
                dma((OUT_BUFS + 1,)),
            ],
            compiler_params=pltpu.CompilerParams(vmem_limit_bytes=16 * 1024 * 1024),
            name="finish",
        )(pre, cnt, shift, therm)
        return therm_out, out.reshape(solutes.shape)

    return jax.shard_map(
        on_device,
        mesh=mesh,
        in_specs=(
            P(None, "gx", "gy"),
            P("gx", "gy"),
            P("gx", "gy"),
            P("gx", "gy", None),
            P("gx", "gy", None),
            P("gx", "gy", None, None),
            P("gx", "gy", None, None, None),
            P(),
        ),
        out_specs=(P(None, "gx", "gy"), P("gx", "gy", None, None, None)),
        check_vma=False,
    )
```

```python
import functools

import jax
import jax.numpy as jnp
from jax import lax
from jax.experimental import pallas as pl
from jax.experimental.pallas import tpu as pltpu
from jax.sharding import PartitionSpec as P

MESH = pl.DeviceIdType.MESH
F32 = jnp.float32
BF16 = jnp.bfloat16

NU_COEF = 0.2
STEP_DT = 0.05
ATTEN_WATER = 0.06
ATTEN_CHL = 0.05
WARMING_SCALE = 0.5
GROWTH_TEMP = 0.063

LEVELS = 32
BLOCKS = 64
UNROLL = 4
LEVEL_STEP = 8
OUT_STEP = 8
OUT_CHUNK = 16
OUT_BUFS = 8
NT = (((1,), (1,)), ((), ()))
TN = (((0,), (0,)), ((), ()))


def iota(shape, dim):
    return lax.broadcasted_iota(jnp.int32, shape, dim)


def one_hot(mask):
    return jnp.where(mask, 1.0, 0.0).astype(BF16)


def swap_chunks(parts):
    lane = iota(parts[0].shape, 1)
    low = lane < 64
    even = (lane & 32) == 0
    a, b, c, d = parts
    a, c = jnp.where(low, a, pltpu.roll(c, 64, 1)), jnp.where(low, pltpu.roll(a, 64, 1), c)
    b, d = jnp.where(low, b, pltpu.roll(d, 64, 1)), jnp.where(low, pltpu.roll(b, 64, 1), d)
    a, b = jnp.where(even, a, pltpu.roll(b, 32, 1)), jnp.where(even, pltpu.roll(a, 96, 1), b)
    c, d = jnp.where(even, c, pltpu.roll(d, 32, 1)), jnp.where(even, pltpu.roll(c, 96, 1), d)
    return [a, b, c, d]


def exchange_kernel(
    gx_n,
    gy_n,
    t_hbm,
    amb_hbm,
    light_hbm,
    flag_hbm,
    tally_hbm,
    hold_hbm,
    rate_hbm,
    c_hbm,
    pre_ref,
    cnt_ref,
    shift_ref,
    therm_ref,
    t_ref,
    amb_ref,
    light_ref,
    flag_ref,
    tally_ref,
    hold_ref,
    rate_ref,
    c_ref,
    sel_ref,
    ut_ref,
    step_ref,
    pay_ref,
    recv_ref,
    ax_ref,
    axr_ref,
    top_ref,
    hs_ref,
    hr_ref,
    tmp_ref,
    heat_ref,
    kap_ref,
    kup_ref,
    gv_ref,
    mix_ref,
    warm_ref,
    hxs_ref,
    hxr_ref,
    hys_ref,
    hyr_ref,
    ar_ref,
    ara_ref,
    arb_ref,
    in_sem,
    c_sem,
    halo_s,
    halo_r,
    xs_sem,
    xr_sem,
    fs_sem,
    fr_sem,
    own_sem,
    bs_sem,
    br_sem,
    as_sem,
    ar_sem,
    gs_sem,
    gr_sem,
):
    nz = gy_n // 4
    mx = lax.axis_index("gx")
    my = lax.axis_index("gy")
    mz = my // 4
    mq = my % 4

    def c_copy(z):
        return pltpu.make_async_copy(
            c_hbm.at[pl.ds(z * 32, 32)], c_ref.at[pl.ds(z * 32, 32)], c_sem.at[z]
        )

    loads = [
        pltpu.make_async_copy(src, dst, in_sem.at[n])
        for n, (src, dst) in enumerate(
            (
                (t_hbm, t_ref),
                (flag_hbm, flag_ref),
                (tally_hbm, tally_ref),
                (hold_hbm, hold_ref),
                (amb_hbm, amb_ref),
                (light_hbm, light_ref),
                (rate_hbm, rate_ref),
            )
        )
    ]
    for copy in loads:
        copy.start()

    bar = pltpu.get_barrier_semaphore()
    for d in range(1, gx_n):
        pl.semaphore_signal(
            bar, 1, device_id={"gx": (mx + d) % gx_n}, device_id_type=MESH
        )
    for d in range(1, gy_n):
        pl.semaphore_signal(
            bar, 1, device_id={"gy": (my + d) % gy_n}, device_id_type=MESH
        )

    for copy in loads:
        copy.wait()
    for q in range(nz):
        c_copy((mz - q + nz) % nz).start()

    dep = (flag_ref[...] * tally_ref[...]).astype(F32)
    hold = hold_ref[...].astype(F32)
    bi = iota((BLOCKS, BLOCKS), 0)
    bj = iota((BLOCKS, BLOCKS), 1)
    hold_b = jnp.broadcast_to(hold, (BLOCKS, BLOCKS))
    hold_c = jnp.sum(jnp.where(bi == bj, hold_b, 0.0), axis=1, keepdims=True)
    same = jnp.where((hold_c == hold_b) & (bi < bj), 1.0, 0.0)
    rank = jnp.sum(same, axis=0, keepdims=True)
    slot = hold * 8.0 + rank
    r8 = iota((8, BLOCKS), 0)
    pair = jnp.where(
        r8 == 0,
        jnp.broadcast_to(slot, (8, BLOCKS)),
        jnp.where(r8 == 1, jnp.broadcast_to(dep, (8, BLOCKS)), 0.0),
    ).astype(BF16)
    spread = one_hot(iota((BLOCKS, 512), 0) == (iota((BLOCKS, 512), 1) >> 3))
    lanes = jnp.dot(pair, spread, preferred_element_type=F32)
    slot_l = lanes[0:1]
    dep_l = lanes[1:2]
    lane8 = iota((8, 128), 1)
    dep_b = [
        jnp.broadcast_to(dep_l[:, 128 * bx : 128 * bx + 128], (8, 128)) for bx in range(4)
    ]
    cells = jnp.sum(dep, axis=1, keepdims=True) * 64.0

    hxs_ref[0, 0:32, :] = t_ref[:, 0, :]
    hxs_ref[1, 0:32, :] = t_ref[:, 31, :]
    hxs_ref[0, 32:40, :] = dep_b[0]
    hxs_ref[1, 32:40, :] = dep_b[3]

    zero8 = jnp.zeros((8, 128), F32)
    low4, high4 = [zero8] * 4, [zero8] * 4
    for k in range(LEVELS):
        for bx in range(4):
            part = t_ref[k, 8 * bx : 8 * bx + 8, :]
            place = 32 * bx + k
            low4[bx] = jnp.where(lane8 == place, pltpu.roll(part, place, 1), low4[bx])
            high4[bx] = jnp.where(
                lane8 == place, pltpu.roll(part, (place + 1) % 128, 1), high4[bx]
            )
    quarter = lane8 >> 5
    low = jnp.where(
        quarter < 2,
        jnp.where(quarter == 0, low4[0], low4[1]),
        jnp.where(quarter == 2, low4[2], low4[3]),
    )
    high = jnp.where(
        quarter < 2,
        jnp.where(quarter == 0, high4[0], high4[1]),
        jnp.where(quarter == 2, high4[2], high4[3]),
    )
    dlow, dhigh = zero8, zero8
    for bx in range(4):
        dlow = jnp.where(lane8 == 32 * bx, pltpu.roll(dep_b[bx], 32 * bx, 1), dlow)
        dhigh = jnp.where(lane8 == 32 * bx, pltpu.roll(dep_b[bx], 32 * bx + 1, 1), dhigh)
    hys_ref[0, 0:8, :] = low
    hys_ref[1, 0:8, :] = high
    hys_ref[0, 8:16, :] = dlow
    hys_ref[1, 8:16, :] = dhigh

    pl.semaphore_wait(bar, gx_n - 1 + gy_n - 1)

    def halo(side):
        step = gx_n - 1 if side == 0 else 1
        stepy = gy_n - 1 if side == 0 else 1
        return (
            pltpu.make_async_remote_copy(
                hxs_ref.at[side],
                hxr_ref.at[1 - side],
                halo_s.at[side],
                halo_r.at[side],
                device_id={"gx": (mx + step) % gx_n},
                device_id_type=MESH,
            ),
            pltpu.make_async_remote_copy(
                hys_ref.at[side],
                hyr_ref.at[1 - side],
                halo_s.at[2 + side],
                halo_r.at[2 + side],
                device_id={"gy": (my + stepy) % gy_n},
                device_id_type=MESH,
            ),
        )

    halos = halo(0) + halo(1)
    for copy in halos:
        copy.start()

    def by_lanes(field):
        return jnp.concatenate([field[8 * bx : 8 * bx + 8] for bx in range(4)], axis=1)

    aux = jnp.concatenate(
        [
            by_lanes(light_ref[...].astype(F32)),
            by_lanes(amb_ref[...].astype(F32)),
            jnp.broadcast_to(dep_l, (8, 512)),
            jnp.zeros((8, 512), F32),
        ],
        axis=0,
    ).astype(BF16)
    er = iota((256, 32), 0)
    ef = iota((256, 32), 1)
    place = one_hot(ef == jnp.where(er < 128, er >> 3, 16))
    wide = jnp.dot(place, aux, preferred_element_type=F32)
    wide = jnp.where(
        (iota((256, 512), 0) & 7) == (iota((256, 512), 1) & 7), wide, 0.0
    ).astype(BF16)
    slots = 8 * gy_n
    sel_b = one_hot(
        iota((slots, 512), 0).astype(F32) == jnp.broadcast_to(slot_l, (slots, 512))
    )
    packed_aux = lax.dot_general(sel_b, wide, NT, preferred_element_type=F32)
    packed_aux = packed_aux.reshape(gy_n, 8, 256)
    ax_ref[...] = jnp.concatenate(
        [packed_aux[:, :, :128], packed_aux[:, :, 128:]], axis=1
    ).astype(BF16)

    def aux_send(other):
        return pltpu.make_async_remote_copy(
            ax_ref.at[other],
            axr_ref.at[my],
            xs_sem.at[other],
            xr_sem.at[my],
            device_id={"gy": other},
            device_id_type=MESH,
        )

    def aux_arrival(other):
        return pltpu.make_async_remote_copy(
            ax_ref.at[other],
            axr_ref.at[other],
            xs_sem.at[other],
            xr_sem.at[other],
            device_id={"gy": other},
            device_id_type=MESH,
        )

    own_aux = pltpu.make_async_copy(ax_ref.at[my], axr_ref.at[my], own_sem.at[2])
    own_aux.start()
    for d in range(1, gy_n):
        aux_send((my + d) % gy_n).start()

    lane_n = iota((1, 512), 1)
    key_l = slot_l * 8.0 + (lane_n & 7).astype(F32)

    def build_sel(z, carry):
        m = iota((256, 1), 0) + z * 256
        key = ((m >> 6) << 6) | ((m & 7) << 3) | ((m >> 3) & 7)
        sel_ref[pl.ds(pl.multiple_of(z * 256, 256), 256), :] = one_hot(
            jnp.broadcast_to(key.astype(F32), (256, 512))
            == jnp.broadcast_to(key_l, (256, 512))
        )
        return carry

    lax.fori_loop(0, nz, build_sel, 0)

    for copy in halos:
        copy.wait_recv()

    row = iota((32, 128), 0)
    lane = iota((32, 128), 1)
    on_low_x = jnp.where(mx > 0, 1.0, 0.0)
    on_high_x = jnp.where(mx < gx_n - 1, 1.0, 0.0)
    on_low_y = jnp.where(my > 0, 1.0, 0.0)
    on_high_y = jnp.where(my < gy_n - 1, 1.0, 0.0)

    def around(field, below_row, above_row, low_h, high_h):
        up = jnp.where(row == 0, below_row, pltpu.roll(field, 1, 0))
        down = jnp.where(row == 31, above_row, pltpu.roll(field, 31, 0))
        low_v = jnp.concatenate(
            [low_h] + [pltpu.roll(low_h, 128 - 32 * bx, 1) for bx in (1, 2, 3)], axis=0
        )
        high_v = jnp.concatenate(
            [pltpu.roll(high_h, 127 - 32 * bx, 1) for bx in range(4)], axis=0
        )
        west = jnp.where(lane == 0, low_v, pltpu.roll(field, 1, 1))
        east = jnp.where(lane == 127, high_v, pltpu.roll(field, 127, 1))
        return up, down, west, east

    dep2 = jnp.concatenate(dep_b, axis=0)
    dep_n = around(
        dep2,
        hxr_ref[0, 32:33, :] * on_low_x,
        hxr_ref[1, 32:33, :] * on_high_x,
        hyr_ref[0, 8:16, :] * on_low_y,
        hyr_ref[1, 8:16, :] * on_high_y,
    )

    def stencil(kk, carry):
        low_h, high_h = carry
        done = []
        for part in range(LEVEL_STEP):
            k = kk * LEVEL_STEP + part
            field = t_ref[k]
            near = around(
                field,
                hxr_ref[0, pl.ds(k, 1), :],
                hxr_ref[1, pl.ds(k, 1), :],
                low_h,
                high_h,
            )
            low_h = pltpu.roll(low_h, 127, 1)
            high_h = pltpu.roll(high_h, 127, 1)
            kf = k.astype(F32)
            total = jnp.where(dep_n[0] > kf, near[0] - field, 0.0)
            for d, n in zip(dep_n[1:], near[1:]):
                total = total + jnp.where(d > kf, n - field, 0.0)
            stepped = field + NU_COEF * jnp.where(dep2 > kf, total, 0.0)
            step_ref[k] = stepped
            done.append(stepped)
        size = 8 * LEVEL_STEP
        rows = pl.ds(pl.multiple_of(kk * size, size), size)
        for bx in range(4):
            ut_ref[rows, 128 * bx : 128 * bx + 128] = jnp.concatenate(
                [d[8 * bx : 8 * bx + 8] for d in done], axis=0
            ).astype(BF16)
        return low_h, high_h

    def forward(other, h):
        rows = pl.ds(h * 64, 64)
        return pltpu.make_async_remote_copy(
            pay_ref.at[other, rows],
            recv_ref.at[my, rows],
            fs_sem.at[h, other],
            fr_sem.at[h, my],
            device_id={"gy": other},
            device_id_type=MESH,
        )

    def arrival(other, h):
        rows = pl.ds(h * 64, 64)
        return pltpu.make_async_remote_copy(
            pay_ref.at[other, rows],
            recv_ref.at[other, rows],
            fs_sem.at[h, other],
            fr_sem.at[h, other],
            device_id={"gy": other},
            device_id_type=MESH,
        )

    own = pltpu.make_async_copy(pay_ref.at[my], recv_ref.at[my], own_sem.at[0])
    edges = (hyr_ref[0, 0:8, :], hyr_ref[1, 0:8, :])
    half_steps = LEVELS // LEVEL_STEP // 2
    for h in range(2):
        edges = lax.fori_loop(h * half_steps, (h + 1) * half_steps, stencil, edges)
        for q in range(nz):
            z = (mz + q) % nz
            part = lax.dot_general(
                sel_ref[pl.ds(pl.multiple_of(z * 256, 256), 256), :],
                ut_ref[h * 128 : h * 128 + 128, :],
                NT,
                preferred_element_type=F32,
            ).astype(BF16)
            pay_ref[pl.ds(z * 4, 4), h * 64 : h * 64 + 64, :] = part.reshape(4, 64, 128)
            for d in range(4):
                if q or d:
                    forward(z * 4 + (mq + d) % 4, h).start()
    own.start()

    pi = iota((256, 256), 0)
    po = iota((256, 256), 1)
    to_columns = one_hot(po == (((pi & 31) << 3) | (pi >> 5)))
    from_columns = one_hot(pi == (((po & 31) << 3) | (po >> 5)))
    rates = jnp.concatenate([rate_ref[...]] * 32, axis=0)
    spread_r = (iota((8, 256), 1) & 7) == iota((8, 256), 0)
    rates_hi = rates.astype(BF16)
    rates_lo = (rates - rates_hi.astype(F32)).astype(BF16)
    spread_r = one_hot(spread_r)
    diagonal = (pi >> 3) == (po >> 3)
    mat_hi = jnp.where(
        diagonal, jnp.dot(rates_hi, spread_r, preferred_element_type=F32), 0.0
    ).astype(BF16)
    mat_lo = jnp.where(
        diagonal, jnp.dot(rates_lo, spread_r, preferred_element_type=F32), 0.0
    ).astype(BF16)
    upper = lane >= 64
    upper8 = lane8 >= 64
    level = jnp.where(upper, 1.0, 0.0)
    sums = (zero8,) * 4

    def back(other):
        return pltpu.make_async_remote_copy(
            hs_ref.at[other],
            hr_ref.at[my],
            bs_sem.at[other],
            br_sem.at[my],
            device_id={"gy": other},
            device_id_type=MESH,
        )

    def back_arrival(other):
        return pltpu.make_async_remote_copy(
            hs_ref.at[other],
            hr_ref.at[other],
            bs_sem.at[other],
            br_sem.at[other],
            device_id={"gy": other},
            device_id_type=MESH,
        )

    own_back = pltpu.make_async_copy(hs_ref.at[my], hr_ref.at[my], own_sem.at[1])

    def gx_send(other):
        return pltpu.make_async_remote_copy(
            ar_ref.at[0],
            ara_ref.at[mx],
            as_sem.at[other],
            ar_sem.at[mx],
            device_id={"gx": other},
            device_id_type=MESH,
        )

    def gx_arrival(other):
        return pltpu.make_async_remote_copy(
            ar_ref.at[0],
            ara_ref.at[other],
            as_sem.at[other],
            ar_sem.at[other],
            device_id={"gx": other},
            device_id_type=MESH,
        )

    def gy_send(other):
        return pltpu.make_async_remote_copy(
            ar_ref.at[1],
            arb_ref.at[my],
            gs_sem.at[other],
            gr_sem.at[my],
            device_id={"gy": other},
            device_id_type=MESH,
        )

    def gy_arrival(other):
        return pltpu.make_async_remote_copy(
            ar_ref.at[1],
            arb_ref.at[other],
            gs_sem.at[other],
            gr_sem.at[other],
            device_id={"gy": other},
            device_id_type=MESH,
        )

    def gx_sums(sums):
        ar_ref[0, 0:8, :] = (sums[0] + sums[1]) + (sums[2] + sums[3])
        ar_ref[0, 8:16, :] = jnp.broadcast_to(cells, (8, 128))
        for d in range(1, gx_n):
            gx_send((mx + d) % gx_n).start()
        ara_ref[mx] = ar_ref[0]

    def row_of(ref, i, s):
        return ref[i, pl.ds(s, 8, stride=0), :]

    def mix_of(i, s):
        return mix_ref[pl.ds(pl.multiple_of(s * 8, 8), 8), 128 * i : 128 * i + 128]

    for q in range(nz):
        z = (mz - q + nz) % nz
        s0 = z * 32
        for d in range(4):
            if q == 0 and d == 0:
                own_aux.wait()
            else:
                aux_arrival(z * 4 + (mq - d + 4) % 4).wait_recv()
        c_copy(z).wait()
        got = axr_ref[pl.ds(z * 4, 4), :, :].astype(F32)
        la = got[:, 0:8, :].reshape(32, 128)
        cnt = got[:, 8:16, :].reshape(32, 128)
        cnt_ref[pl.ds(s0, 32), :] = cnt
        light = jnp.where(upper, pltpu.roll(la, 64, 1), la)
        run = jnp.zeros((32, 128), F32)
        prev = light
        wet = cnt - level
        for i in range(16):
            at = slice(128 * i, 128 * i + 128)
            atten = ATTEN_WATER + ATTEN_CHL * c_ref[pl.ds(s0, 32), 0, at]
            both = atten + pltpu.roll(atten, 64, 1)
            cum = run + jnp.where(upper, both, atten)
            run = run + both
            bottom = light * jnp.exp(-cum)
            bottom_r = pltpu.roll(bottom, 64, 1)
            top = jnp.where(upper, bottom_r, prev)
            prev = bottom_r
            top_ref[i, pl.ds(s0, 32), :] = top
            heat_ref[:, at] = jnp.where(wet > 2.0 * i, top - bottom, 0.0)
        for g in range(8):
            at = slice(256 * g, 256 * g + 256)
            c_b = c_ref[pl.ds(s0, 32), :, at].reshape(256, 256).astype(BF16)
            mix_ref[pl.ds(pl.multiple_of(s0 * 8, 256), 256), at] = jnp.dot(mat_hi, c_b, preferred_element_type=F32) + jnp.dot(
                mat_lo, c_b, preferred_element_type=F32
            )

        heat = jnp.concatenate(
            [heat_ref[:, g * 256 : g * 256 + 256] for g in range(8)], axis=0
        ).astype(BF16)
        back_cols = jnp.dot(heat, from_columns, preferred_element_type=F32)
        for h in range(2):
            quads = [
                swap_chunks(
                    [
                        back_cols[
                            (h * 4 + g) * 32 : (h * 4 + g) * 32 + 32, yh * 128 : yh * 128 + 128
                        ]
                        for g in range(4)
                    ]
                )
                for yh in range(2)
            ]
            flat = [p.reshape(4, 8, 128) for p in quads[0] + quads[1]]
            for y in range(0, 8, 2):
                hs_ref[pl.ds(z * 4, 4), h * 64 + y * 8 : h * 64 + y * 8 + 16, :] = (
                    jnp.concatenate([flat[y], flat[y + 1]], axis=1).astype(BF16)
                )
    for q in range(nz):
        z = (mz - q + nz) % nz
        s0 = z * 32
        for d in range(4):
            if q == 0 and d == 0:
                own.wait()
            else:
                arrival(z * 4 + (mq - d + 4) % 4, 0).wait_recv()
                arrival(z * 4 + (mq - d + 4) % 4, 1).wait_recv()
        blk = recv_ref[pl.ds(z * 4, 4), :, :].astype(F32)
        rows = []
        for h in range(2):
            quads = []
            for yh in range(2):
                quads.append(
                    swap_chunks(
                        [
                            blk[:, h * 64 + y * 8 : h * 64 + y * 8 + 8, :].reshape(32, 128)
                            for y in range(yh * 4, yh * 4 + 4)
                        ]
                    )
                )
            for g in range(4):
                rows.append(jnp.concatenate([quads[0][g], quads[1][g]], axis=1))
        cols = jnp.dot(
            jnp.concatenate(rows, axis=0).astype(BF16),
            to_columns,
            preferred_element_type=F32,
        )
        for g in range(8):
            tmp_ref[pl.ds(s0, 32), g * 256 : g * 256 + 256] = cols[g * 32 : g * 32 + 32]

        wet = cnt_ref[pl.ds(s0, 32), :] - level
        for i in range(16):
            at = slice(128 * i, 128 * i + 128)
            top = top_ref[i, pl.ds(s0, 32), :]
            growth = jnp.exp(GROWTH_TEMP * tmp_ref[pl.ds(s0, 32), at]) * top / (top + 1.0)
            gv_ref[i, pl.ds(s0, 32)] = jnp.where(wet > 2.0 * i, STEP_DT * growth, 0.0)

        def grow(step, acc):
            acc = list(acc)
            for u in range(UNROLL):
                s = s0 + step * UNROLL + u
                for i in range(16):
                    acc[i % 4] = acc[i % 4] + row_of(gv_ref, i, s) * mix_of(i, s)
            return tuple(acc)

        sums = lax.fori_loop(0, 32 // UNROLL, grow, sums)
    gx_sums(sums)

    own_back.start()
    for d in range(1, gy_n):
        back((my + d) % gy_n).start()

    def diffusion(z):
        s0 = z * 32
        la = axr_ref[pl.ds(z * 4, 4), 0:8, :].astype(F32).reshape(32, 128)
        amb = jnp.where(upper, la, pltpu.roll(la, 64, 1))
        wet = cnt_ref[pl.ds(s0, 32), :] - level
        kap_prev = jnp.zeros((32, 128), F32)
        t_next = tmp_ref[pl.ds(s0, 32), 0:128]
        tr_next = pltpu.roll(t_next, 64, 1)
        for i in range(16):
            t_i, tr_i = t_next, tr_next
            if i < 15:
                t_next = tmp_ref[pl.ds(s0, 32), 128 * i + 128 : 128 * i + 256]
                tr_next = pltpu.roll(t_next, 64, 1)
                t_below = jnp.where(upper, tr_next, tr_i)
            else:
                t_below = jnp.where(upper, t_i, tr_i)
            kap = amb * (1.0 + 0.5 * jnp.tanh(t_i - t_below))
            kap = jnp.where(wet > 2.0 * i + 1.0, STEP_DT * kap, 0.0)
            kap_r = pltpu.roll(kap, 64, 1)
            kap_ref[i, pl.ds(s0, 32)] = kap
            kup_ref[i, pl.ds(s0, 32)] = jnp.where(upper, kap_r, kap_prev)
            kap_prev = kap_r

    for z in range(nz):
        diffusion(z)

    def tracers(step, carry):
        for u in range(UNROLL):
            s = step * UNROLL + u
            c_next = c_ref[s, :, 0:128]
            cr_next = pltpu.roll(c_next, 64, 1)
            cr_i = cr_next
            for i in range(16):
                at = slice(128 * i, 128 * i + 128)
                cr_prev = cr_i
                c_i, cr_i = c_next, cr_next
                if i < 15:
                    c_next = c_ref[s, :, 128 * i + 128 : 128 * i + 256]
                    cr_next = pltpu.roll(c_next, 64, 1)
                below = jnp.where(upper8, cr_next, cr_i)
                above = jnp.where(upper8, cr_i, cr_prev)
                grown = row_of(gv_ref, i, s) * mix_of(i, s)
                pre_ref[s, :, at] = (c_i + row_of(kap_ref, i, s) * (below - c_i)) + (
                    row_of(kup_ref, i, s) * (above - c_i) + grown
                )
        return carry

    steps = slots // UNROLL
    lax.fori_loop(0, steps // 4, tracers, 0)
    for d in range(1, gx_n):
        gx_arrival((mx + d) % gx_n).wait_recv()
    ar_ref[1] = jnp.sum(ara_ref[...], axis=0)
    for d in range(1, gy_n):
        gy_send((my + d) % gy_n).start()
    arb_ref[my] = ar_ref[1]
    lax.fori_loop(steps // 4, steps, tracers, 0)

    for q in range(nz):
        z = (mz + q) % nz
        for d in range(4):
            if q == 0 and d == 0:
                own_back.wait()
            else:
                back_arrival(z * 4 + (mq + d) % 4).wait_recv()
        got = hr_ref[pl.ds(z * 4, 4), :, :]
        sel = sel_ref[pl.ds(pl.multiple_of(z * 256, 256), 256), :]
        for h in range(2):
            lhs = got[:, h * 64 : h * 64 + 64, :].reshape(256, 128)
            warm = lax.dot_general(lhs, sel, TN, preferred_element_type=F32)
            rows_h = slice(128 * h, 128 * h + 128)
            if q == 0:
                warm_ref[rows_h, :] = warm
            else:
                warm_ref[rows_h, :] = warm_ref[rows_h, :] + warm

    def finish(k, carry):
        part = warm_ref[pl.ds(pl.multiple_of(k * 8, 8), 8), :]
        for bx in range(4):
            therm_ref[k, 8 * bx : 8 * bx + 8, :] = (
                step_ref[k, 8 * bx : 8 * bx + 8, :]
                + WARMING_SCALE * part[:, 128 * bx : 128 * bx + 128]
            )
        return carry

    lax.fori_loop(0, LEVELS, finish, 0)

    for copy in halos:
        copy.wait_send()
    for d in range(1, gy_n):
        forward((my + d) % gy_n, 0).wait_send()
        forward((my + d) % gy_n, 1).wait_send()
        back((my + d) % gy_n).wait_send()
        aux_send((my + d) % gy_n).wait_send()
    for d in range(1, gx_n):
        gx_send((mx + d) % gx_n).wait_send()

    for d in range(1, gy_n):
        gy_arrival((my + d) % gy_n).wait_recv()
    total = jnp.sum(arb_ref[...], axis=0)
    grown = jnp.sum(total[0:8], axis=1, keepdims=True)
    shift_ref[...] = -(jnp.broadcast_to(grown, (8, 128)) / jnp.maximum(total[8:16], 1.0))

    for d in range(1, gy_n):
        gy_send((my + d) % gy_n).wait_send()


def finish_kernel(pre_ref, cnt_ref, shift_ref, therm_ref, out_ref, thout_ref, buf_ref, sem):
    level = jnp.where(iota((8, 128), 1) >= 64, 1.0, 0.0)
    n = pre_ref.shape[0] // OUT_CHUNK
    thermal = pltpu.make_async_copy(therm_ref, thout_ref, sem.at[OUT_BUFS])
    thermal.start()
    shift = shift_ref[...]

    def out_copy(c):
        return pltpu.make_async_copy(
            buf_ref.at[c % OUT_BUFS],
            out_ref.at[pl.ds(c * OUT_CHUNK, OUT_CHUNK)],
            sem.at[c % OUT_BUFS],
        )

    for c in range(n):
        if c >= OUT_BUFS:
            out_copy(c - OUT_BUFS).wait()

        def some(step, carry):
            for u in range(OUT_STEP):
                s = step * OUT_STEP + u
                wet = cnt_ref[pl.ds(c * OUT_CHUNK + s, 8, stride=0), :] - level
                for i in range(16):
                    at = slice(128 * i, 128 * i + 128)
                    buf_ref[c % OUT_BUFS, s, :, at] = pre_ref[
                        c * OUT_CHUNK + s, :, at
                    ] + jnp.where(wet > 2.0 * i, shift, 0.0)
            return carry

        lax.fori_loop(0, OUT_CHUNK // OUT_STEP, some, 0)
        out_copy(c).start()
    for c in range(max(n - OUT_BUFS, 0), n):
        out_copy(c).wait()
    thermal.wait()


def solution(mesh):
    gx_n = mesh.shape["gx"]
    gy_n = mesh.shape["gy"]
    slots = 8 * gy_n

    def on_device(thermal, amb, light, flags, tally, hold, solutes, rates):
        dma = pltpu.SemaphoreType.DMA
        vmem = pl.BlockSpec(memory_space=pltpu.VMEM)
        hbm = pl.BlockSpec(memory_space=pltpu.HBM)
        tracers = solutes.reshape(slots, 8, 2048)
        pre, cnt, shift, therm = pl.pallas_call(
            functools.partial(exchange_kernel, gx_n, gy_n),
            out_shape=[
                pltpu.VMEM((slots, 8, 2048), F32),
                pltpu.VMEM((slots + 8, 128), F32),
                pltpu.VMEM((8, 128), F32),
                pltpu.VMEM((32, 32, 128), F32),
            ],
            in_specs=[hbm] * 8,
            out_specs=[vmem] * 4,
            scratch_shapes=[
                pltpu.VMEM((32, 32, 128), F32),
                pltpu.VMEM((32, 128), BF16),
                pltpu.VMEM((32, 128), BF16),
                pltpu.VMEM((1, BLOCKS), jnp.int32),
                pltpu.VMEM((1, BLOCKS), jnp.int32),
                pltpu.VMEM((1, BLOCKS), jnp.int32),
                pltpu.VMEM((8, 8), F32),
                pltpu.VMEM((slots, 8, 2048), F32),
                pltpu.VMEM((64 * gy_n, 512), BF16),
                pltpu.VMEM((256, 512), BF16),
                pltpu.VMEM((32, 32, 128), F32),
                pltpu.VMEM((gy_n, 128, 128), BF16),
                pltpu.VMEM((gy_n, 128, 128), BF16),
                pltpu.VMEM((gy_n, 16, 128), BF16),
                pltpu.VMEM((gy_n, 16, 128), BF16),
                pltpu.VMEM((16, slots, 128), F32),
                pltpu.VMEM((gy_n, 128, 128), BF16),
                pltpu.VMEM((gy_n, 128, 128), BF16),
                pltpu.VMEM((slots, 2048), F32),
                pltpu.VMEM((32, 2048), F32),
                pltpu.VMEM((16, slots + 8, 128), F32),
                pltpu.VMEM((16, slots + 8, 128), F32),
                pltpu.VMEM((16, slots + 8, 128), F32),
                pltpu.VMEM((8 * slots, 2048), F32),
                pltpu.VMEM((256, 512), F32),
                pltpu.VMEM((2, 40, 128), F32),
                pltpu.VMEM((2, 40, 128), F32),
                pltpu.VMEM((2, 16, 128), F32),
                pltpu.VMEM((2, 16, 128), F32),
                pltpu.VMEM((2, 16, 128), F32),
                pltpu.VMEM((gx_n, 16, 128), F32),
                pltpu.VMEM((gy_n, 16, 128), F32),
                dma((7,)),
                dma((gy_n // 4,)),
                dma((4,)),
                dma((4,)),
                dma((gy_n,)),
                dma((gy_n,)),
                dma((2, gy_n)),
                dma((2, gy_n)),
                dma((3,)),
                dma((gy_n,)),
                dma((gy_n,)),
                dma((gx_n,)),
                dma((gx_n,)),
                dma((gy_n,)),
                dma((gy_n,)),
            ],
            compiler_params=pltpu.CompilerParams(
                collective_id=0, has_side_effects=True, vmem_limit_bytes=40 * 1024 * 1024
            ),
            name="exchange",
        )(
            *(
                pltpu.with_memory_space_constraint(a, pltpu.HBM)
                for a in (
                    thermal,
                    amb,
                    light,
                    flags.reshape(1, BLOCKS),
                    tally.reshape(1, BLOCKS),
                    hold.reshape(1, BLOCKS),
                    rates,
                    tracers,
                )
            )
        )
        out, therm_out = pl.pallas_call(
            finish_kernel,
            out_shape=[
                jax.ShapeDtypeStruct((slots, 8, 2048), F32),
                jax.ShapeDtypeStruct((32, 32, 128), F32),
            ],
            in_specs=[vmem] * 4,
            out_specs=[hbm] * 2,
            scratch_shapes=[
                pltpu.VMEM((OUT_BUFS, OUT_CHUNK, 8, 2048), F32),
                dma((OUT_BUFS + 1,)),
            ],
            compiler_params=pltpu.CompilerParams(vmem_limit_bytes=16 * 1024 * 1024),
            name="finish",
        )(pre, cnt, shift, therm)
        return therm_out, out.reshape(solutes.shape)

    return jax.shard_map(
        on_device,
        mesh=mesh,
        in_specs=(
            P(None, "gx", "gy"),
            P("gx", "gy"),
            P("gx", "gy"),
            P("gx", "gy", None),
            P("gx", "gy", None),
            P("gx", "gy", None, None),
            P("gx", "gy", None, None, None),
            P(),
        ),
        out_specs=(P(None, "gx", "gy"), P("gx", "gy", None, None, None)),
        check_vma=False,
    )
```
